32 devices in a mesh: seq: 8 (over z, y), head: 4 (over x, core).
Axes of the slice: x: 2, y: 2, z: 4, core: 2. Of those that a mesh axis runs over, the one named last changes fastest.
Arguments:
- inputs: bfloat16 [2048, 2560], P('seq', 'head'), may hold values from -6 to 6
- step_sizes: float32 [40, 2048], P('head', 'seq'), may hold values from 0.1 to 1
- input_map: bfloat16 [2048, 128], P('seq'), may hold values from -1.78125 to 1.78125
- output_map: bfloat16 [2048, 128], P('seq'), may hold values from -1.78125 to 1.78125
- level_table: float32 [40, 2, 12], P('head'), may hold values from 0.25 to 2
- token_class: int32 [2048], P('seq'), may hold values from 0 to 1
- cotangent: bfloat16 [2048, 2560], P('seq', 'head'), may hold values from -6 to 6
Outputs:
- layer_out: bfloat16 [2048, 2560], P('seq', 'head')
- input_grad: bfloat16 [2048, 2560], P('seq', 'head')
- step_grad: float32 [40, 2048], P('head', 'seq')
- input_map_grad: float32 [2048, 128], P('seq')
- output_map_grad: float32 [2048, 128], P('seq')
- table_grad: float32 [40, 2, 12], P('head')
The draws below stay inside these ranges and needn't reach their ends.
All inputs are finite; a program needn't handle non-finite values.
Results may differ from the reference program's by a relative error of at most 0.006.
Values may be sent and summed in bfloat16 or wider, within the bound.
A program may use at most 64 MiB of HBM per device.

```python
import math
import jax
import jax.numpy as jnp
from jax import lax

H = 40
P_SIZE = 64
N = 128
Q = 128
CLASSES = 2
TOK_DEV = 256
TOKENS = 2048
TOK_BITS = 8
STRETCH_BITS = 7
LEVELS = 12
N_SEQ = 8


def plant(drawn, rng, low, largest):
    longest = drawn.shape.index(max(drawn.shape))
    spots = []
    for shift in (0, 1):
        where = [jax.random.randint(jax.random.fold_in(rng, axis), (), 0, length) for axis, length in enumerate(drawn.shape)]
        where[longest] = (where[longest] + shift) % drawn.shape[longest]
        spots.append(tuple(where))
    return drawn.at[spots[0]].set(low).at[spots[1]].set(largest)


def levels(rng, dims, split, low, largest):
    level, own = 1.0, jax.random.fold_in(rng, 6)
    for dim, blocks in split:
        heights = jnp.exp(jax.random.uniform(jax.random.fold_in(own, dim), (blocks,), jnp.float32, low / len(split), largest / len(split)))
        level = level * jnp.repeat(heights, dims[dim] // blocks).reshape([-1 if axis == dim else 1 for axis in range(len(dims))])
    return level


def bell_draw(own_key, extent, spread, limit, shards=(), held_as=jnp.bfloat16):
    array = jax.random.normal(own_key, extent, jnp.float32) * spread
    if len(shards) > 0:
        array = levels(own_key, extent, shards, -0.22, 0.18) * array
    return jnp.clip(array, min=-limit, max=limit).astype(held_as)


def setup_inputs(seed: int = 0) -> dict:
    keys = jax.random.split(jax.random.key(seed), 8)
    inputs = bell_draw(keys[0], (TOKENS, H * P_SIZE), 1.0, 6.0, ((0, 8), (1, 4)))
    step_sizes = jnp.clip(jnp.exp(math.log(1.0) - 2.3025851 * jax.random.uniform(keys[1], (H, TOKENS), jnp.float32) ** levels(keys[1], (H, TOKENS), ((0, 4), (1, 8)), -0.2, 0.2)), 0.1, 1.0)
    input_map = bell_draw(keys[2], (TOKENS, N), (N ** -0.25), 1.78125, ((0, 8),))
    output_map = bell_draw(keys[3], (TOKENS, N), (N ** -0.25), 1.78125, ((0, 8),))
    level_table = jnp.clip(jnp.exp(math.log(2.0) - 2.0794415 * jax.random.uniform(keys[4], (H, CLASSES, LEVELS), jnp.float32) ** levels(keys[4], (H, CLASSES, LEVELS), ((0, 4),), -0.2, 0.2)), 0.25, 2.0)
    token_class = plant(jax.random.randint(keys[5], (TOKENS,), 0, CLASSES), jax.random.fold_in(keys[5], 1), 0, CLASSES - 1).astype(jnp.int32)
    cotangent = bell_draw(keys[6], (TOKENS, H * P_SIZE), 1.0, 6.0, ((0, 8), (1, 4)))
    return dict(inputs=inputs, step_sizes=step_sizes, input_map=input_map, output_map=output_map, level_table=level_table, token_class=token_class, cotangent=cotangent)


highest = lax.Precision.HIGHEST

def level_of(differ, bit_count):
    result = jnp.zeros(differ.shape, jnp.int32)
    for bit_index in range(bit_count):
        result = result + (differ >= 1 << bit_index).astype(jnp.int32)
    return result

def level_scale(level_count):
    ladder = jnp.arange(level_count).astype(jnp.float32)
    return jnp.where(ladder > 0, jnp.exp2(-0.5 * (ladder - 1.0)), 1.0).astype(jnp.float32)

def rounded(value):
    return lax.optimization_barrier(value.astype(jnp.bfloat16)).astype(jnp.float32)

def reference(inputs, step_sizes, input_map, output_map, level_table, token_class, cotangent):
    stretch_count = TOKENS // Q
    per_device = TOK_DEV // Q
    position = jnp.arange(Q, dtype=jnp.int32)
    near = level_of(position[:, None] ^ position[None, :], STRETCH_BITS)
    causal = position[:, None] >= position[None, :]
    near_onehot = jnp.stack([(near == level_index) & causal for level_index in range(STRETCH_BITS + 1)]).astype(jnp.float32)
    scales = level_scale(LEVELS)
    class_onehot = (token_class[:, None] == jnp.arange(CLASSES, dtype=jnp.int32)[None, :]).astype(jnp.float32)
    class_stretches = class_onehot.reshape(stretch_count, Q, CLASSES)
    class_first = jnp.transpose(class_stretches, (2, 0, 1))
    map_in = input_map.reshape(stretch_count, Q, N).astype(jnp.float32)
    map_out = output_map.reshape(stretch_count, Q, N).astype(jnp.float32)
    scores = jnp.einsum('ctn,csn->cts', map_out, map_in, precision=highest)
    head_inputs = jnp.transpose(inputs.reshape(TOKENS, H, P_SIZE), (1, 0, 2))
    head_grads = jnp.transpose(cotangent.reshape(TOKENS, H, P_SIZE), (1, 0, 2))

    def per_head(carry, packed):
        head_in, head_cot, head_step, head_table = packed
        values = head_in.reshape(stretch_count, Q, P_SIZE).astype(jnp.float32)
        grads = head_cot.reshape(stretch_count, Q, P_SIZE).astype(jnp.float32)
        step_stretches = head_step.reshape(stretch_count, Q)
        weighted = head_table * scales[None, :]
        coeff = jnp.dot(class_onehot, weighted[:, :STRETCH_BITS + 1], precision=highest).reshape(stretch_count, Q, STRETCH_BITS + 1)
        weight = jnp.einsum('ctl,lts->cts', coeff, near_onehot, precision=highest)
        mixing = rounded(scores * weight * step_stretches[:, None, :])
        intra_out = jnp.einsum('cts,csp->ctp', mixing, values, precision=highest)
        scaled_in = rounded(values * step_stretches[:, :, None])
        stretch_state = jnp.einsum('csp,csn->cpn', scaled_in, map_in, precision=highest)
        block_state = rounded(stretch_state.reshape(N_SEQ, per_device, P_SIZE, N).sum(axis=1))
        masked = grads[None] * class_first[:, :, :, None]
        query_state = jnp.einsum('kctp,ctn->kcpn', masked, map_out, precision=highest)
        query_block = query_state.reshape(CLASSES, N_SEQ, per_device, P_SIZE, N).sum(axis=2)
        class_state = jnp.zeros((CLASSES, stretch_count, P_SIZE, N), jnp.float32)
        source_state = jnp.zeros((stretch_count, P_SIZE, N), jnp.float32)
        far_grad = []
        for level_index in range(STRETCH_BITS + 1, LEVELS):
            if level_index <= TOK_BITS:
                span = 2 ** (level_index - 1 - STRETCH_BITS)
                unit = 1
                source_base = stretch_state
                query_base = query_state
            else:
                span = 2 ** (level_index - 1 - TOK_BITS)
                unit = per_device
                source_base = block_state
                query_base = query_block
            blocks = source_base.reshape(-1, span, P_SIZE, N).sum(axis=1)
            query_blocks = query_base.reshape(CLASSES, -1, span, P_SIZE, N).sum(axis=2)
            odd = (jnp.arange(blocks.shape[0]) % 2 == 1)[:, None, None]
            earlier = jnp.concatenate([jnp.zeros_like(blocks[:1]), blocks[:-1]], axis=0)
            later = jnp.concatenate([query_blocks[:, 1:], jnp.zeros_like(query_blocks[:, :1])], axis=1)
            segment = jnp.repeat(jnp.where(odd, earlier, 0.0), span * unit, axis=0)
            back = jnp.repeat(jnp.where(odd[None], 0.0, later), span * unit, axis=1)
            class_state = class_state + weighted[:, level_index][:, None, None, None] * segment[None]
            source_state = source_state + jnp.einsum('k,kcpn->cpn', weighted[:, level_index], back, precision=highest)
            far_grad.append(scales[level_index] * lax.optimization_barrier(jnp.sum(segment[None] * query_state, axis=(1, 2, 3))))
        class_round = rounded(class_state)
        reads = jnp.einsum('ctn,kcpn->kctp', map_out, class_round, precision=highest)
        far_out = lax.optimization_barrier(jnp.sum(class_first[:, :, :, None] * reads, axis=0))
        layer = (intra_out + far_out).astype(jnp.bfloat16).reshape(TOKENS, P_SIZE)
        source_round = rounded(source_state)
        value_grad = jnp.einsum('csn,cpn->csp', map_in, source_round, precision=highest)
        mix_grad = jnp.einsum('ctp,csp->cts', grads, values, precision=highest)
        score_grad = rounded(mix_grad * weight * step_stretches[:, None, :])
        back_values = jnp.einsum('cts,ctp->csp', mixing, grads, precision=highest)
        input_grad = (back_values + step_stretches[:, :, None] * value_grad).astype(jnp.bfloat16).reshape(TOKENS, P_SIZE)
        step_grad = (lax.optimization_barrier(jnp.sum(mix_grad * scores * weight, axis=1)) + lax.optimization_barrier(jnp.sum(values * value_grad, axis=2))).reshape(TOKENS)
        map_in_grad = jnp.einsum('cts,ctn->csn', score_grad, map_out, precision=highest) + jnp.einsum('csp,cpn->csn', scaled_in, source_round, precision=highest)
        out_reads = jnp.einsum('ctp,kcpn->kctn', grads, class_round, precision=highest)
        map_out_grad = jnp.einsum('cts,csn->ctn', score_grad, map_in, precision=highest) + lax.optimization_barrier(jnp.sum(class_first[:, :, :, None] * out_reads, axis=0))
        near_terms = mix_grad * scores * step_stretches[:, None, :]
        per_level = jnp.einsum('cts,lts->ctl', near_terms, near_onehot, precision=highest)
        near_grad = jnp.einsum('ctk,ctl->kl', class_stretches, per_level, precision=highest) * scales[None, :STRETCH_BITS + 1]
        table_grad = jnp.concatenate([near_grad, jnp.stack(far_grad, axis=1)], axis=1) / jnp.sqrt(jnp.float32(TOKENS))
        new_carry = (carry[0] + map_in_grad.reshape(TOKENS, N), carry[1] + map_out_grad.reshape(TOKENS, N))
        return (new_carry, (layer, input_grad, step_grad, table_grad))
    zeros = jnp.zeros((TOKENS, N), jnp.float32)
    sums, stacked = lax.scan(per_head, (zeros, zeros), (head_inputs, head_grads, step_sizes, level_table))
    layer_out = jnp.transpose(stacked[0], (1, 0, 2)).reshape(TOKENS, H * P_SIZE)
    input_grad = jnp.transpose(stacked[1], (1, 0, 2)).reshape(TOKENS, H * P_SIZE)
    return (layer_out, input_grad, stacked[2], sums[0], sums[1], stacked[3])
```

```python
import functools
import math

import jax
import jax.numpy as jnp
from jax import lax
from jax.experimental import pallas as pl
from jax.experimental.pallas import tpu as pltpu
from jax.sharding import PartitionSpec as P

Q = 128
LANES = 128
F32 = jnp.float32
BF16 = jnp.bfloat16
HIGH = lax.Precision.HIGHEST
MESH = pl.DeviceIdType.MESH


def dot(a, b, ca, cb, precision=None):
    return lax.dot_general(
        a, b, (((ca,), (cb,)), ((), ())), precision=precision, preferred_element_type=F32
    )


def scale_of(level):
    return 1.0 if level == 0 else 2.0 ** (-(level - 1) / 2)


def kernel(
    dims,
    x_ref,
    step_ref,
    bin_ref,
    cout_ref,
    table_ref,
    class_ref,
    g_ref,
    out_ref,
    xg_ref,
    sg_ref,
    ing_ref,
    outg_ref,
    tg_ref,
    stepx,
    scaled,
    clsb,
    lev,
    scores,
    mo2,
    s0,
    q1,
    qown,
    frun,
    rrun,
    fcs,
    fsrc,
    nout,
    nback,
    score_sum,
    in_acc,
    out_acc,
    tab,
    send_f,
    recv_f,
    send_r,
    recv_r,
    part_send,
    part_recv,
    part_own,
    final,
    tsend,
    trecv,
    f_ssem,
    f_rsem,
    r_ssem,
    r_rsem,
    p_ssem,
    p_rsem,
    a_ssem,
    a_rsem,
    t_ssem,
    t_rsem,
    steprow,
    sgrow,
):
    heads, width, tokens, state, levels, nb, n_head, total = dims
    per = LANES // width
    pairs = heads // per
    sb = Q.bit_length() - 1
    mid = sb + 1
    far0 = mid + 1
    device = lax.axis_index("seq")
    mine = lax.axis_index("head")

    barrier = pltpu.get_barrier_semaphore()
    for b in range(nb):
        pl.semaphore_signal(barrier, inc=1, device_id={"seq": device ^ (1 << b)}, device_id_type=MESH)
    for i in range(1, n_head):
        pl.semaphore_signal(
            barrier, inc=1, device_id={"head": lax.rem(mine + i, n_head)}, device_id_type=MESH
        )

    lane = lax.broadcasted_iota(jnp.int32, (1, LANES), 1)
    halves = [(lane // width == j) for j in range(per)]
    half_f = [m.astype(F32) for m in halves]
    half_b = [m.astype(F32).astype(BF16) for m in halves]
    zero = jnp.zeros((state, LANES), F32)

    def wrow(p, k, level):
        row = jnp.zeros((1, LANES), F32)
        for j in range(per):
            row = jnp.where(halves[j], table_ref[p * per + j, k, level] * scale_of(level), row)
        return row

    def cols(p):
        return pl.ds(pl.multiple_of(p * LANES, LANES), LANES)

    row = class_ref[...].astype(F32)
    clsb[...] = dot(
        jnp.broadcast_to(row, (16, tokens)).astype(BF16),
        jnp.full((16, LANES), 0.0625, BF16),
        0,
        0,
    )
    t_id = lax.broadcasted_iota(jnp.int32, (Q, Q), 0)
    s_id = lax.broadcasted_iota(jnp.int32, (Q, Q), 1)
    differ = t_id ^ s_id
    level_id = jnp.zeros((Q, Q), jnp.int32)
    for bit in range(sb):
        level_id = level_id + (differ >= (1 << bit)).astype(jnp.int32)
    lev[...] = jnp.where(t_id >= s_id, level_id, -1)
    spans = [slice(c * Q, (c + 1) * Q) for c in range(2)]
    for c in range(2):
        scores[c] = dot(cout_ref[spans[c], :], bin_ref[spans[c], :], 1, 1)
        one = clsb[spans[c], :]
        mo = cout_ref[spans[c], :].astype(F32)
        mo2[c, :, :state] = (mo * (1.0 - one)).astype(BF16)
        mo2[c, :, state:] = (mo * one).astype(BF16)
    for h in range(heads):
        for c in range(2):
            steprow[h, c : c + 1, :] = step_ref[h : h + 1, spans[c]]
    score_sum[...] = jnp.zeros_like(score_sum)
    in_acc[...] = jnp.zeros_like(in_acc)
    out_acc[...] = jnp.zeros_like(out_acc)
    tab[...] = jnp.zeros_like(tab)

    def f_copy(b, p):
        return pltpu.make_async_remote_copy(
            send_f.at[b, p], recv_f.at[b, p], f_ssem.at[b, p], f_rsem.at[b, p],
            device_id={"seq": device ^ (1 << b)}, device_id_type=MESH,
        )

    def r_copy(b, k, p):
        return pltpu.make_async_remote_copy(
            send_r.at[b, k, p], recv_r.at[b, k, p], r_ssem.at[b, k, p], r_rsem.at[b, k, p],
            device_id={"seq": device ^ (1 << b)}, device_id_type=MESH,
        )

    bit_of = [(device >> b) & 1 for b in range(nb)]
    above = [device >> (b + 1) for b in range(nb)]
    ones = [(1 << (nb - b - 1)) - 1 for b in range(nb)]
    f_sent = [(bit_of[b] == 0) | (above[b] != ones[b]) for b in range(nb)]
    f_came = [(bit_of[b] == 1) | (above[b] != ones[b]) for b in range(nb)]
    c_sent = [(bit_of[b] == 1) & (above[b] == 0) for b in range(nb)]
    c_came = [(bit_of[b] == 0) & (above[b] == 0) for b in range(nb)]
    r_both = [above[b] != 0 for b in range(nb)]

    def start(b, p):
        @pl.when(f_sent[b])
        def _():
            send_f[b, p] = frun[p].astype(BF16)
            f_copy(b, p).start()

        @pl.when(c_sent[b])
        def _():
            send_r[b, 0, p] = (
                wrow(p, 0, far0 + b) * rrun[0, p] + wrow(p, 1, far0 + b) * rrun[1, p]
            ).astype(BF16)
            r_copy(b, 0, p).start()

        @pl.when(r_both[b])
        def _():
            for k in range(2):
                send_r[b, k, p] = rrun[k, p].astype(BF16)
                r_copy(b, k, p).start()

    def put_rows(k, level, p, value):
        for j in range(per):
            tab[k * levels + level, pl.ds(p * per + j, 1), :] = value * half_f[j]

    def combine(b, p):
        @pl.when(f_came[b])
        def _():
            f_copy(b, p).wait_recv()
            got = recv_f[b, p].astype(F32)
            frun[p] = frun[p] + got

        @pl.when(bit_of[b] == 1)
        def _():
            got = recv_f[b, p].astype(F32)
            for k in range(2):
                fcs[k, p] = fcs[k, p] + wrow(p, k, far0 + b) * got
                put_rows(k, far0 + b, p, jnp.sum(got * qown[k, p], axis=0, keepdims=True))

        @pl.when(c_came[b])
        def _():
            r_copy(b, 0, p).wait_recv()
            fsrc[p] = fsrc[p] + recv_r[b, 0, p].astype(F32)

        @pl.when(r_both[b])
        def _():
            for k in range(2):
                r_copy(b, k, p).wait_recv()
                got = recv_r[b, k, p].astype(F32)
                rrun[k, p] = rrun[k, p] + got

            @pl.when(bit_of[b] == 0)
            def _():
                fsrc[p] = (
                    fsrc[p]
                    + wrow(p, 0, far0 + b) * recv_r[b, 0, p].astype(F32)
                    + wrow(p, 1, far0 + b) * recv_r[b, 1, p].astype(F32)
                )

    def states(p, carry):
        picks = (
            lax.broadcasted_iota(jnp.int32, (heads, LANES), 0)
            == p * per + lax.broadcasted_iota(jnp.int32, (heads, LANES), 1) // width
        ).astype(F32)
        grown = dot(step_ref[...], picks, 0, 0, HIGH)
        stepx[p] = grown
        sc = (x_ref[:, cols(p)].astype(F32) * grown).astype(BF16)
        scaled[p] = sc
        st = [dot(bin_ref[spans[c], :], sc[spans[c]], 0, 0) for c in range(2)]
        s0[p] = st[0]
        frun[p] = st[0] + st[1]
        q = [dot(mo2[c], g_ref[spans[c], cols(p)], 0, 0) for c in range(2)]
        for k in range(2):
            part = [q[c][k * state : (k + 1) * state] for c in range(2)]
            q1[k, p] = part[1]
            both = part[0] + part[1]
            qown[k, p] = both
            rrun[k, p] = both
            fcs[k, p] = zero
            put_rows(k, mid, p, jnp.sum(st[0] * part[1], axis=0, keepdims=True))
        fsrc[p] = zero
        return carry

    def begin(p, carry):
        start(0, p)
        return carry

    def states_begin(p, carry):
        states(p, carry)
        return begin(p, carry)

    pl.semaphore_wait(barrier, nb + n_head - 1)
    lax.fori_loop(0, pairs, states_begin, 0)

    def near(p, carry):
        lv = lev[...]
        hit = [lv == level for level in range(sb + 1)]
        weights = []
        for j in range(per):
            rows = []
            for k in range(2):
                acc = jnp.zeros((Q, Q), F32)
                for level in range(sb + 1):
                    acc = jnp.where(
                        hit[level], table_ref[p * per + j, k, level] * scale_of(level), acc
                    )
                rows.append(acc)
            weights.append(rows)
        terms = [[jnp.zeros((Q, Q), F32) for k in range(2)] for j in range(per)]
        for c in range(2):
            x = x_ref[spans[c], cols(p)]
            g = g_ref[spans[c], cols(p)]
            xs = jnp.concatenate([x * half_b[j] for j in range(per)], axis=0)
            gs = jnp.concatenate([g * half_b[j] for j in range(per)], axis=0)
            mg = dot(gs, x, 1, 1)
            is_one = clsb[spans[c], :] > 0.5
            score = scores[c]
            mixes = []
            total_sg = score_sum[c]
            for j in range(per):
                head = p * per + j
                step = steprow[head, c : c + 1, :]
                weight = jnp.where(is_one, weights[j][1], weights[j][0])
                ws = weight * step
                mgj = mg[j * Q : (j + 1) * Q]
                mixes.append((score * ws).astype(BF16))
                total_sg = total_sg + mgj * ws
                graded = mgj * score
                sgrow[head, c : c + 1, :] = jnp.sum(graded * weight, axis=0, keepdims=True)
                term = graded * step
                terms[j][0] = terms[j][0] + jnp.where(is_one, 0.0, term)
                terms[j][1] = terms[j][1] + jnp.where(is_one, term, 0.0)
            score_sum[c] = total_sg
            nout[p, spans[c], :] = dot(jnp.concatenate(mixes, axis=1), xs, 1, 0)
            nback[p, spans[c], :] = dot(jnp.concatenate(mixes, axis=0), gs, 0, 0)
        for j in range(per):
            for k in range(2):
                term = terms[j][k]
                for level in range(sb + 1):
                    if level <= 3:
                        value = jnp.sum(jnp.where(hit[level], term, 0.0), axis=0, keepdims=True)
                    else:
                        size = 1 << (level - 1)
                        value = jnp.zeros((1, LANES), F32)
                        for odd in range(1, Q // size, 2):
                            rows = jnp.sum(term[odd * size : (odd + 1) * size], axis=0, keepdims=True)
                            value = jnp.where(lane // size == odd - 1, rows, value)
                    tab[k * levels + level, pl.ds(p * per + j, 1), :] = value
        return carry

    def near_combine(p, carry):
        near(p, carry)
        combine(0, p)
        if nb > 1:
            start(1, p)
        return carry

    lax.fori_loop(0, pairs, near_combine, 0)

    for b in range(1, nb):
        def step_b(p, carry, b=b):
            combine(b, p)
            if b + 1 < nb:
                start(b + 1, p)
            return carry

        lax.fori_loop(0, pairs, step_b, 0)

    def table_copy(b):
        return pltpu.make_async_remote_copy(
            tsend.at[b], trecv.at[b], t_ssem.at[b], t_rsem.at[b],
            device_id={"seq": device ^ (1 << b)}, device_id_type=MESH,
        )

    table_sum = []
    for k in range(2):
        acc = jnp.zeros((heads, LANES), F32)
        for level in range(levels):
            col = jnp.sum(tab[k * levels + level], axis=1, keepdims=True)
            acc = jnp.where(lane == level, col * (scale_of(level) / math.sqrt(total)), acc)
        table_sum.append(acc)
    for k in range(2):
        tsend[0, k, :heads, :] = table_sum[k]
    table_copy(0).start()

    def far(p, carry):
        for c in range(2):
            cs = []
            for k in range(2):
                value = fcs[k, p]
                if c == 1:
                    value = value + wrow(p, k, mid) * s0[p]
                cs.append(value.astype(BF16))
            cs = jnp.concatenate(cs, axis=0)
            src = fsrc[p]
            if c == 0:
                src = src + wrow(p, 0, mid) * q1[0, p] + wrow(p, 1, mid) * q1[1, p]
            src = src.astype(BF16)
            read = dot(mo2[c], cs, 1, 0)
            out_ref[spans[c], cols(p)] = (nout[p, spans[c], :] + read).astype(BF16)
            vg = dot(bin_ref[spans[c], :], src, 1, 0)
            xg_ref[spans[c], cols(p)] = (
                nback[p, spans[c], :] + stepx[p, spans[c], :] * vg
            ).astype(BF16)
            picks = jnp.concatenate(half_f + [jnp.zeros((8 - per, LANES), F32)], axis=0)
            far_step = dot(picks, x_ref[spans[c], cols(p)].astype(F32) * vg, 1, 1, HIGH)
            for j in range(per):
                at = (p * per + j, slice(c, c + 1), slice(None))
                sgrow[at] = sgrow[at] + far_step[j : j + 1]
            in_acc[c] = in_acc[c] + dot(scaled[p, spans[c], :], src, 1, 1)
            out_acc[c] = out_acc[c] + dot(g_ref[spans[c], cols(p)], cs, 1, 1)
        return carry

    lax.fori_loop(0, pairs, far, 0)

    for h in range(heads):
        for c in range(2):
            sg_ref[h : h + 1, spans[c]] = sgrow[h, c : c + 1, :]

    grads = [[], []]
    for c in range(2):
        sgb = score_sum[c].astype(BF16)
        is_one = clsb[spans[c], :] > 0.5
        acc = out_acc[c]
        grads[0].append(in_acc[c] + dot(sgb, cout_ref[spans[c], :], 0, 0))
        grads[1].append(
            jnp.where(is_one, acc[:, state:], acc[:, :state])
            + dot(sgb, bin_ref[spans[c], :], 1, 0)
        )
    full = jnp.concatenate(grads[0] + grads[1], axis=0)
    rows = 2 * tokens // n_head
    for q in range(n_head):
        part_own[q] = full[q * rows : (q + 1) * rows]
        part_send[q] = full[q * rows : (q + 1) * rows].astype(BF16)

    def part_copy(i):
        to = lax.rem(mine + i, n_head)
        return pltpu.make_async_remote_copy(
            part_send.at[to], part_recv.at[i], p_ssem.at[i], p_rsem.at[i],
            device_id={"head": to}, device_id_type=MESH,
        )

    def all_copy(i, slot):
        to = lax.rem(mine + i, n_head)
        return pltpu.make_async_remote_copy(
            final.at[slot], final.at[slot], a_ssem.at[i], a_rsem.at[i],
            device_id={"head": to}, device_id_type=MESH,
        )

    for i in range(1, n_head):
        part_copy(i).start()
    for b in range(nb):
        table_copy(b).wait_recv()
        for k in range(2):
            table_sum[k] = table_sum[k] + trecv[b, k, :heads, :]
        if b + 1 < nb:
            for k in range(2):
                tsend[b + 1, k, :heads, :] = table_sum[k]
            table_copy(b + 1).start()
        if b == 0:
            summed = part_own[mine]
            for i in range(1, n_head):
                part_copy(i).wait_recv()
                summed = summed + part_recv[i].astype(F32)
            final[mine] = summed.astype(BF16)
            for i in range(1, n_head):
                all_copy(i, mine).start()
    for k in range(2):
        tg_ref[:, k, :] = table_sum[k][:, :levels]
    for i in range(1, n_head):
        all_copy(i, lax.rem(mine + n_head - i, n_head)).wait_recv()
    per_out = n_head // 2
    for q in range(n_head):
        where = (slice((q % per_out) * rows, (q % per_out + 1) * rows), slice(None))
        (ing_ref if q < per_out else outg_ref)[where] = final[q].astype(F32)

    for i in range(1, n_head):
        part_copy(i).wait_send()
        all_copy(i, mine).wait_send()
    for b in range(nb):
        table_copy(b).wait_send()

        def drain(p, carry, b=b):
            @pl.when(f_sent[b])
            def _():
                f_copy(b, p).wait_send()

            @pl.when(c_sent[b])
            def _():
                r_copy(b, 0, p).wait_send()

            @pl.when(r_both[b])
            def _():
                for k in range(2):
                    r_copy(b, k, p).wait_send()

            return carry

        lax.fori_loop(0, pairs, drain, 0)


def local(inputs, step_sizes, input_map, output_map, level_table, token_class, cotangent):
    tokens, state = input_map.shape
    heads = step_sizes.shape[0]
    width = inputs.shape[1] // heads
    levels = level_table.shape[2]
    n_seq = lax.axis_size("seq")
    n_head = lax.axis_size("head")
    nb = n_seq.bit_length() - 1
    per = LANES // width
    pairs = heads // per
    assert tokens == 2 * Q and heads % per == 0 and n_head % 2 == 0 and nb > 0
    assert level_table.shape[1] == 2 and state == Q
    dims = (heads, width, tokens, state, levels, nb, n_head, float(tokens * n_seq))
    rows = 2 * tokens // n_head
    vmem = pl.BlockSpec(memory_space=pltpu.VMEM)
    smem = pl.BlockSpec(memory_space=pltpu.SMEM)
    dma = pltpu.SemaphoreType.DMA
    unit = (pairs, state, LANES)
    tall = (pairs, tokens, LANES)
    padded = -(-heads // 8) * 8
    return pl.pallas_call(
        functools.partial(kernel, dims),
        out_shape=(
            jax.ShapeDtypeStruct(inputs.shape, BF16),
            jax.ShapeDtypeStruct(inputs.shape, BF16),
            jax.ShapeDtypeStruct(step_sizes.shape, F32),
            jax.ShapeDtypeStruct(input_map.shape, F32),
            jax.ShapeDtypeStruct(output_map.shape, F32),
            jax.ShapeDtypeStruct(level_table.shape, F32),
        ),
        in_specs=[vmem, vmem, vmem, vmem, smem, vmem, vmem],
        out_specs=(vmem,) * 6,
        scratch_shapes=[
            pltpu.VMEM(tall, F32),
            pltpu.VMEM(tall, BF16),
            pltpu.VMEM((tokens, LANES), F32),
            pltpu.VMEM((Q, Q), jnp.int32),
            pltpu.VMEM((2, Q, Q), F32),
            pltpu.VMEM((2, Q, 2 * state), BF16),
            pltpu.VMEM(unit, F32),
            pltpu.VMEM((2, *unit), F32),
            pltpu.VMEM((2, *unit), F32),
            pltpu.VMEM(unit, F32),
            pltpu.VMEM((2, *unit), F32),
            pltpu.VMEM((2, *unit), F32),
            pltpu.VMEM(unit, F32),
            pltpu.VMEM(tall, F32),
            pltpu.VMEM(tall, F32),
            pltpu.VMEM((2, Q, Q), F32),
            pltpu.VMEM((2, Q, state), F32),
            pltpu.VMEM((2, Q, 2 * state), F32),
            pltpu.VMEM((2 * levels, heads, LANES), F32),
            pltpu.VMEM((nb, *unit), BF16),
            pltpu.VMEM((nb, *unit), BF16),
            pltpu.VMEM((nb, 2, *unit), BF16),
            pltpu.VMEM((nb, 2, *unit), BF16),
            pltpu.VMEM((n_head, rows, state), BF16),
            pltpu.VMEM((n_head, rows, state), BF16),
            pltpu.VMEM((n_head, rows, state), F32),
            pltpu.VMEM((n_head, rows, state), BF16),
            pltpu.VMEM((nb, 2, padded, LANES), F32),
            pltpu.VMEM((nb, 2, padded, LANES), F32),
            dma((nb, pairs)),
            dma((nb, pairs)),
            dma((nb, 2, pairs)),
            dma((nb, 2, pairs)),
            dma((n_head,)),
            dma((n_head,)),
            dma((n_head,)),
            dma((n_head,)),
            dma((nb,)),
            dma((nb,)),
            pltpu.VMEM((heads, 2, LANES), F32),
            pltpu.VMEM((heads, 2, LANES), F32),
        ],
        compiler_params=pltpu.CompilerParams(
            collective_id=0, has_side_effects=True, vmem_limit_bytes=48 << 20
        ),
    )(
        inputs, step_sizes, input_map, output_map, level_table,
        token_class.reshape(1, tokens), cotangent,
    )


def solution(mesh):
    placed = (
        P("seq", "head"),
        P("head", "seq"),
        P("seq", None),
        P("seq", None),
        P("head", None, None),
        P("seq"),
        P("seq", "head"),
    )
    return jax.shard_map(
        local,
        mesh=mesh,
        in_specs=placed,
        out_specs=(
            P("seq", "head"),
            P("seq", "head"),
            P("head", "seq"),
            P("seq", None),
            P("seq", None),
            P("head", None, None),
        ),
        check_vma=False,
    )
```

```python
import functools
import math

import jax
import jax.numpy as jnp
from jax import lax
from jax.experimental import pallas as pl
from jax.experimental.pallas import tpu as pltpu
from jax.sharding import PartitionSpec as P

Q = 128
LANES = 128
F32 = jnp.float32
BF16 = jnp.bfloat16
HIGH = lax.Precision.HIGHEST
MESH = pl.DeviceIdType.MESH


def dot(a, b, ca, cb, precision=None):
    return lax.dot_general(
        a, b, (((ca,), (cb,)), ((), ())), precision=precision, preferred_element_type=F32
    )


def scale_of(level):
    return 1.0 if level == 0 else 2.0 ** (-(level - 1) / 2)


def kernel(
    dims,
    x_hbm,
    step_hbm,
    bin_hbm,
    cout_hbm,
    table_ref,
    class_hbm,
    g_hbm,
    out_ref,
    xg_ref,
    sg_ref,
    ing_ref,
    outg_ref,
    tg_ref,
    stepx,
    scaled,
    clsb,
    lev,
    scores,
    mo2,
    s0,
    q1,
    qown,
    frun,
    rrun,
    fcs,
    fsrc,
    nout,
    nback,
    score_sum,
    in_acc,
    out_acc,
    tab,
    send_f,
    recv_f,
    send_r,
    recv_r,
    part_send,
    part_recv,
    part_own,
    final,
    tsend,
    trecv,
    f_ssem,
    f_rsem,
    r_ssem,
    r_rsem,
    p_ssem,
    p_rsem,
    a_ssem,
    a_rsem,
    t_ssem,
    t_rsem,
    steprow,
    sgrow,
    class_b,
    source_b,
    x_ref,
    step_ref,
    bin_ref,
    cout_ref,
    class_ref,
    g_ref,
    in_sem,
):
    heads, width, tokens, state, levels, nb, n_head, total = dims
    per = LANES // width
    pairs = heads // per
    sb = Q.bit_length() - 1
    mid = sb + 1
    far0 = mid + 1
    device = lax.axis_index("seq")
    mine = lax.axis_index("head")

    barrier = pltpu.get_barrier_semaphore()
    for b in range(nb):
        pl.semaphore_signal(barrier, inc=1, device_id={"seq": device ^ (1 << b)}, device_id_type=MESH)
    for i in range(1, n_head):
        pl.semaphore_signal(
            barrier, inc=1, device_id={"head": lax.rem(mine + i, n_head)}, device_id_type=MESH
        )

    loads = [
        pltpu.make_async_copy(src, dst, in_sem.at[i])
        for i, (src, dst) in enumerate(
            [
                (class_hbm, class_ref),
                (cout_hbm, cout_ref),
                (bin_hbm, bin_ref),
                (step_hbm, step_ref),
                (x_hbm, x_ref),
                (g_hbm, g_ref),
            ]
        )
    ]
    for load in loads:
        load.start()

    lane = lax.broadcasted_iota(jnp.int32, (1, LANES), 1)
    halves = [(lane // width == j) for j in range(per)]
    half_f = [m.astype(F32) for m in halves]
    half_b = [m.astype(F32).astype(BF16) for m in halves]
    zero = jnp.zeros((state, LANES), F32)

    def wrow(p, k, level):
        row = jnp.zeros((1, LANES), F32)
        for j in range(per):
            row = jnp.where(halves[j], table_ref[p * per + j, k, level] * scale_of(level), row)
        return row

    def cols(p):
        return pl.ds(pl.multiple_of(p * LANES, LANES), LANES)

    for load in loads:
        load.wait()
    row = class_ref[...].astype(F32)
    clsb[...] = dot(
        jnp.broadcast_to(row, (16, tokens)).astype(BF16),
        jnp.full((16, LANES), 0.0625, BF16),
        0,
        0,
    )
    t_id = lax.broadcasted_iota(jnp.int32, (Q, Q), 0)
    s_id = lax.broadcasted_iota(jnp.int32, (Q, Q), 1)
    differ = t_id ^ s_id
    level_id = jnp.zeros((Q, Q), jnp.int32)
    for bit in range(sb):
        level_id = level_id + (differ >= (1 << bit)).astype(jnp.int32)
    lev[...] = jnp.where(t_id >= s_id, level_id, -1)
    spans = [slice(c * Q, (c + 1) * Q) for c in range(2)]
    for c in range(2):
        scores[c] = dot(cout_ref[spans[c], :], bin_ref[spans[c], :], 1, 1)
        one = clsb[spans[c], :]
        mo = cout_ref[spans[c], :].astype(F32)
        mo2[c, :, :state] = (mo * (1.0 - one)).astype(BF16)
        mo2[c, :, state:] = (mo * one).astype(BF16)
    for h in range(heads):
        for c in range(2):
            steprow[h, c : c + 1, :] = step_ref[h : h + 1, spans[c]]
    score_sum[...] = jnp.zeros_like(score_sum)
    in_acc[...] = jnp.zeros_like(in_acc)
    out_acc[...] = jnp.zeros_like(out_acc)
    tab[...] = jnp.zeros_like(tab)

    def f_copy(b, p):
        return pltpu.make_async_remote_copy(
            send_f.at[b, p], recv_f.at[b, p], f_ssem.at[b, p], f_rsem.at[b, p],
            device_id={"seq": device ^ (1 << b)}, device_id_type=MESH,
        )

    def r_copy(b, k, p):
        return pltpu.make_async_remote_copy(
            send_r.at[b, k, p], recv_r.at[b, k, p], r_ssem.at[b, k, p], r_rsem.at[b, k, p],
            device_id={"seq": device ^ (1 << b)}, device_id_type=MESH,
        )

    bit_of = [(device >> b) & 1 for b in range(nb)]
    above = [device >> (b + 1) for b in range(nb)]
    ones = [(1 << (nb - b - 1)) - 1 for b in range(nb)]
    f_sent = [(bit_of[b] == 0) | (above[b] != ones[b]) for b in range(nb)]
    f_came = [(bit_of[b] == 1) | (above[b] != ones[b]) for b in range(nb)]
    count = [sum(bit_of[b + 1 :], jnp.int32(0)) for b in range(nb)]
    c_sent = [(bit_of[b] == 1) & (count[b] <= 1) for b in range(nb)]
    c_came = [(bit_of[b] == 0) & (count[b] <= 1) for b in range(nb)]
    r_none = [count[b] == 0 for b in range(nb)]
    r_one = [count[b] == 1 for b in range(nb)]
    r_both = [count[b] >= 2 for b in range(nb)]

    def combined(p, level_row):
        return level_row(0) * rrun[0, p] + level_row(1) * rrun[1, p]

    def start(b, p):
        @pl.when(f_sent[b])
        def _():
            send_f[b, p] = frun[p].astype(BF16)
            f_copy(b, p).start()

        @pl.when(c_sent[b])
        def _():
            def now():
                return combined(p, lambda k: wrow(p, k, far0 + b)).astype(BF16)

            if b == 0:
                send_r[b, 0, p] = now()
            else:

                @pl.when(r_one[b])
                def _():
                    send_r[b, 0, p] = now()

                @pl.when(r_none[b])
                def _():
                    send_r[b, 0, p] = rrun[0, p].astype(BF16)

            r_copy(b, 0, p).start()

        @pl.when(r_one[b])
        def _():
            def later(k):
                row = wrow(p, k, far0 + nb - 1)
                for other in range(b + 1, nb - 1):
                    row = jnp.where(bit_of[other] == 1, wrow(p, k, far0 + other), row)
                return row

            if b == 0:
                rrun[0, p] = combined(p, later)
            else:

                @pl.when(bit_of[b] == 1)
                def _():
                    rrun[0, p] = combined(p, later)

            send_r[b, 1, p] = rrun[0, p].astype(BF16)
            r_copy(b, 1, p).start()

        @pl.when(r_both[b])
        def _():
            for k in range(2):
                send_r[b, k, p] = rrun[k, p].astype(BF16)
                r_copy(b, k, p).start()

    def put_rows(k, level, p, value):
        for j in range(per):
            tab[k * levels + level, pl.ds(p * per + j, 1), :] = value * half_f[j]

    def combine(b, p):
        @pl.when(f_came[b])
        def _():
            f_copy(b, p).wait_recv()
            got = recv_f[b, p].astype(F32)
            frun[p] = frun[p] + got

        @pl.when(bit_of[b] == 1)
        def _():
            got = recv_f[b, p].astype(F32)
            for k in range(2):
                fcs[k, p] = fcs[k, p] + wrow(p, k, far0 + b) * got
                put_rows(k, far0 + b, p, jnp.sum(got * qown[k, p], axis=0, keepdims=True))

        @pl.when(c_came[b])
        def _():
            r_copy(b, 0, p).wait_recv()
            fsrc[p] = fsrc[p] + recv_r[b, 0, p].astype(F32)

        @pl.when(r_one[b])
        def _():
            r_copy(b, 1, p).wait_recv()
            rrun[0, p] = rrun[0, p] + recv_r[b, 1, p].astype(F32)

        @pl.when(r_both[b])
        def _():
            for k in range(2):
                r_copy(b, k, p).wait_recv()
                got = recv_r[b, k, p].astype(F32)
                rrun[k, p] = rrun[k, p] + got

            @pl.when(bit_of[b] == 0)
            def _():
                fsrc[p] = (
                    fsrc[p]
                    + wrow(p, 0, far0 + b) * recv_r[b, 0, p].astype(F32)
                    + wrow(p, 1, far0 + b) * recv_r[b, 1, p].astype(F32)
                )

    def states(p, carry):
        picks = (
            lax.broadcasted_iota(jnp.int32, (heads, LANES), 0)
            == p * per + lax.broadcasted_iota(jnp.int32, (heads, LANES), 1) // width
        ).astype(F32)
        grown = dot(step_ref[...], picks, 0, 0, HIGH)
        stepx[p] = grown
        sc = (x_ref[:, cols(p)].astype(F32) * grown).astype(BF16)
        scaled[p] = sc
        st = [dot(bin_ref[spans[c], :], sc[spans[c]], 0, 0) for c in range(2)]
        s0[p] = st[0]
        frun[p] = st[0] + st[1]
        q = [dot(mo2[c], g_ref[spans[c], cols(p)], 0, 0) for c in range(2)]
        for k in range(2):
            part = [q[c][k * state : (k + 1) * state] for c in range(2)]
            q1[k, p] = part[1]
            both = part[0] + part[1]
            qown[k, p] = both
            rrun[k, p] = both
            fcs[k, p] = zero
            put_rows(k, mid, p, jnp.sum(st[0] * part[1], axis=0, keepdims=True))
        fsrc[p] = zero
        return carry

    def begin(p, carry):
        start(0, p)
        return carry

    def states_begin(p, carry):
        states(p, carry)
        return begin(p, carry)

    pl.semaphore_wait(barrier, nb + n_head - 1)
    lax.fori_loop(0, pairs, states_begin, 0)

    def near(p, carry):
        lv = lev[...]
        hit = [lv == level for level in range(sb + 1)]
        weights = []
        for j in range(per):
            rows = []
            for k in range(2):
                acc = jnp.zeros((Q, Q), F32)
                for level in range(sb + 1):
                    acc = jnp.where(
                        hit[level], table_ref[p * per + j, k, level] * scale_of(level), acc
                    )
                rows.append(acc)
            weights.append(rows)
        terms = [[jnp.zeros((Q, Q), F32) for k in range(2)] for j in range(per)]
        for c in range(2):
            x = x_ref[spans[c], cols(p)]
            g = g_ref[spans[c], cols(p)]
            xs = jnp.concatenate([x * half_b[j] for j in range(per)], axis=0)
            gs = jnp.concatenate([g * half_b[j] for j in range(per)], axis=0)
            mg = dot(gs, x, 1, 1)
            is_one = clsb[spans[c], :] > 0.5
            score = scores[c]
            mixes = []
            total_sg = score_sum[c]
            for j in range(per):
                head = p * per + j
                step = steprow[head, c : c + 1, :]
                weight = jnp.where(is_one, weights[j][1], weights[j][0])
                ws = weight * step
                mgj = mg[j * Q : (j + 1) * Q]
                mixes.append((score * ws).astype(BF16))
                total_sg = total_sg + mgj * ws
                graded = mgj * score
                sgrow[head, c : c + 1, :] = jnp.sum(graded * weight, axis=0, keepdims=True)
                term = graded * step
                terms[j][0] = terms[j][0] + jnp.where(is_one, 0.0, term)
                terms[j][1] = terms[j][1] + jnp.where(is_one, term, 0.0)
            score_sum[c] = total_sg
            nout[p, spans[c], :] = dot(jnp.concatenate(mixes, axis=1), xs, 1, 0)
            nback[p, spans[c], :] = dot(jnp.concatenate(mixes, axis=0), gs, 0, 0)
        for j in range(per):
            for k in range(2):
                term = terms[j][k]
                for level in range(sb + 1):
                    if level <= 3:
                        value = jnp.sum(jnp.where(hit[level], term, 0.0), axis=0, keepdims=True)
                    else:
                        size = 1 << (level - 1)
                        value = jnp.zeros((1, LANES), F32)
                        for odd in range(1, Q // size, 2):
                            rows = jnp.sum(term[odd * size : (odd + 1) * size], axis=0, keepdims=True)
                            value = jnp.where(lane // size == odd - 1, rows, value)
                    tab[k * levels + level, pl.ds(p * per + j, 1), :] = value
        return carry

    def far_maps(p):
        for c in range(2):
            cs = []
            for k in range(2):
                value = fcs[k, p]
                if c == 1:
                    value = value + wrow(p, k, mid) * s0[p]
                cs.append(value.astype(BF16))
            cs = jnp.concatenate(cs, axis=0)
            src = fsrc[p]
            if c == 0:
                src = src + wrow(p, 0, mid) * q1[0, p] + wrow(p, 1, mid) * q1[1, p]
            src = src.astype(BF16)
            class_b[c, p] = cs
            source_b[c, p] = src
            in_acc[c] = in_acc[c] + dot(scaled[p, spans[c], :], src, 1, 1)
            out_acc[c] = out_acc[c] + dot(g_ref[spans[c], cols(p)], cs, 1, 1)

    def far_values(p):
        for c in range(2):
            cs = class_b[c, p]
            src = source_b[c, p]
            read = dot(mo2[c], cs, 1, 0)
            out_ref[spans[c], cols(p)] = (nout[p, spans[c], :] + read).astype(BF16)
            vg = dot(bin_ref[spans[c], :], src, 1, 0)
            xg_ref[spans[c], cols(p)] = (
                nback[p, spans[c], :] + stepx[p, spans[c], :] * vg
            ).astype(BF16)
            picks = jnp.concatenate(half_f + [jnp.zeros((8 - per, LANES), F32)], axis=0)
            far_step = dot(picks, x_ref[spans[c], cols(p)].astype(F32) * vg, 1, 1, HIGH)
            for j in range(per):
                at = (p * per + j, slice(c, c + 1), slice(None))
                sgrow[at] = sgrow[at] + far_step[j : j + 1]

    lag = 2

    def pipeline(i, carry):
        last = i - lag * (nb - 1)

        @pl.when(last > 0)
        def _():
            far_values(last - 1)

        @pl.when(i < pairs)
        def _():
            near(i, 0)

        for b in range(nb):
            p = i - lag * b

            @pl.when((p >= 0) & (p < pairs))
            def _(b=b, p=p):
                combine(b, p)
                if b + 1 < nb:
                    start(b + 1, p)
                else:
                    far_maps(p)

        return carry

    lax.fori_loop(0, pairs + lag * (nb - 1), pipeline, 0)

    grads = [[], []]
    for c in range(2):
        sgb = score_sum[c].astype(BF16)
        is_one = clsb[spans[c], :] > 0.5
        acc = out_acc[c]
        grads[0].append(in_acc[c] + dot(sgb, cout_ref[spans[c], :], 0, 0))
        grads[1].append(
            jnp.where(is_one, acc[:, state:], acc[:, :state])
            + dot(sgb, bin_ref[spans[c], :], 1, 0)
        )
    full = jnp.concatenate(grads[0] + grads[1], axis=0)
    rows = 2 * tokens // n_head
    for q in range(n_head):
        part_own[q] = full[q * rows : (q + 1) * rows]
        part_send[q] = full[q * rows : (q + 1) * rows].astype(BF16)

    def part_copy(i):
        to = lax.rem(mine + i, n_head)
        return pltpu.make_async_remote_copy(
            part_send.at[to], part_recv.at[i], p_ssem.at[i], p_rsem.at[i],
            device_id={"head": to}, device_id_type=MESH,
        )

    def all_copy(i, slot):
        to = lax.rem(mine + i, n_head)
        return pltpu.make_async_remote_copy(
            final.at[slot], final.at[slot], a_ssem.at[i], a_rsem.at[i],
            device_id={"head": to}, device_id_type=MESH,
        )

    for i in range(1, n_head):
        part_copy(i).start()
    def table_copy(b):
        return pltpu.make_async_remote_copy(
            tsend.at[b], trecv.at[b], t_ssem.at[b], t_rsem.at[b],
            device_id={"seq": device ^ (1 << b)}, device_id_type=MESH,
        )

    table_sum = []
    for k in range(2):
        acc = jnp.zeros((heads, LANES), F32)
        for level in range(levels):
            col = jnp.sum(tab[k * levels + level], axis=1, keepdims=True)
            acc = jnp.where(lane == level, col * (scale_of(level) / math.sqrt(total)), acc)
        table_sum.append(acc)
    for k in range(2):
        tsend[0, k, :heads, :] = table_sum[k]
    table_copy(0).start()

    far_values(pairs - 1)
    for h in range(heads):
        for c in range(2):
            sg_ref[h : h + 1, spans[c]] = sgrow[h, c : c + 1, :]
    for b in range(nb):
        table_copy(b).wait_recv()
        for k in range(2):
            table_sum[k] = table_sum[k] + trecv[b, k, :heads, :]
        if b + 1 < nb:
            for k in range(2):
                tsend[b + 1, k, :heads, :] = table_sum[k]
            table_copy(b + 1).start()
        if b == 0:
            summed = part_own[mine]
            for i in range(1, n_head):
                part_copy(i).wait_recv()
                summed = summed + part_recv[i].astype(F32)
            final[mine] = summed.astype(BF16)
            for i in range(1, n_head):
                all_copy(i, mine).start()
    for k in range(2):
        tg_ref[:, k, :] = table_sum[k][:, :levels]
    for i in range(1, n_head):
        all_copy(i, lax.rem(mine + n_head - i, n_head)).wait_recv()
    per_out = n_head // 2
    for q in range(n_head):
        where = (slice((q % per_out) * rows, (q % per_out + 1) * rows), slice(None))
        (ing_ref if q < per_out else outg_ref)[where] = final[q].astype(F32)

    for i in range(1, n_head):
        part_copy(i).wait_send()
        all_copy(i, mine).wait_send()
    for b in range(nb):
        table_copy(b).wait_send()

        def drain(p, carry, b=b):
            @pl.when(f_sent[b])
            def _():
                f_copy(b, p).wait_send()

            @pl.when(c_sent[b])
            def _():
                r_copy(b, 0, p).wait_send()

            @pl.when(r_one[b])
            def _():
                r_copy(b, 1, p).wait_send()

            @pl.when(r_both[b])
            def _():
                for k in range(2):
                    r_copy(b, k, p).wait_send()

            return carry

        lax.fori_loop(0, pairs, drain, 0)


def write_out(*refs):
    sem = refs[-1]
    copies = [pltpu.make_async_copy(refs[i], refs[6 + i], sem.at[i]) for i in range(6)]
    for copy in copies:
        copy.start()
    for copy in copies:
        copy.wait()


def local(inputs, step_sizes, input_map, output_map, level_table, token_class, cotangent):
    tokens, state = input_map.shape
    heads = step_sizes.shape[0]
    width = inputs.shape[1] // heads
    levels = level_table.shape[2]
    n_seq = lax.axis_size("seq")
    n_head = lax.axis_size("head")
    nb = n_seq.bit_length() - 1
    per = LANES // width
    pairs = heads // per
    assert tokens == 2 * Q and heads % per == 0 and n_head % 2 == 0 and nb > 0
    assert level_table.shape[1] == 2 and state == Q
    dims = (heads, width, tokens, state, levels, nb, n_head, float(tokens * n_seq))
    rows = 2 * tokens // n_head
    vmem = pl.BlockSpec(memory_space=pltpu.VMEM)
    hbm = pl.BlockSpec(memory_space=pltpu.HBM)
    smem = pl.BlockSpec(memory_space=pltpu.SMEM)
    dma = pltpu.SemaphoreType.DMA
    unit = (pairs, state, LANES)
    tall = (pairs, tokens, LANES)
    padded = -(-heads // 8) * 8
    results = pl.pallas_call(
        functools.partial(kernel, dims),
        out_shape=(
            jax.ShapeDtypeStruct(inputs.shape, BF16),
            jax.ShapeDtypeStruct(inputs.shape, BF16),
            jax.ShapeDtypeStruct(step_sizes.shape, F32),
            jax.ShapeDtypeStruct(input_map.shape, F32),
            jax.ShapeDtypeStruct(output_map.shape, F32),
            jax.ShapeDtypeStruct(level_table.shape, F32),
        ),
        in_specs=[hbm, hbm, hbm, hbm, smem, hbm, hbm],
        out_specs=(vmem,) * 6,
        scratch_shapes=[
            pltpu.VMEM(tall, F32),
            pltpu.VMEM(tall, BF16),
            pltpu.VMEM((tokens, LANES), F32),
            pltpu.VMEM((Q, Q), jnp.int32),
            pltpu.VMEM((2, Q, Q), F32),
            pltpu.VMEM((2, Q, 2 * state), BF16),
            pltpu.VMEM(unit, F32),
            pltpu.VMEM((2, *unit), F32),
            pltpu.VMEM((2, *unit), F32),
            pltpu.VMEM(unit, F32),
            pltpu.VMEM((2, *unit), F32),
            pltpu.VMEM((2, *unit), F32),
            pltpu.VMEM(unit, F32),
            pltpu.VMEM(tall, F32),
            pltpu.VMEM(tall, F32),
            pltpu.VMEM((2, Q, Q), F32),
            pltpu.VMEM((2, Q, state), F32),
            pltpu.VMEM((2, Q, 2 * state), F32),
            pltpu.VMEM((2 * levels, heads, LANES), F32),
            pltpu.VMEM((nb, *unit), BF16),
            pltpu.VMEM((nb, *unit), BF16),
            pltpu.VMEM((nb, 2, *unit), BF16),
            pltpu.VMEM((nb, 2, *unit), BF16),
            pltpu.VMEM((n_head, rows, state), BF16),
            pltpu.VMEM((n_head, rows, state), BF16),
            pltpu.VMEM((n_head, rows, state), F32),
            pltpu.VMEM((n_head, rows, state), BF16),
            pltpu.VMEM((nb, 2, padded, LANES), F32),
            pltpu.VMEM((nb, 2, padded, LANES), F32),
            dma((nb, pairs)),
            dma((nb, pairs)),
            dma((nb, 2, pairs)),
            dma((nb, 2, pairs)),
            dma((n_head,)),
            dma((n_head,)),
            dma((n_head,)),
            dma((n_head,)),
            dma((nb,)),
            dma((nb,)),
            pltpu.VMEM((heads, 2, LANES), F32),
            pltpu.VMEM((heads, 2, LANES), F32),
            pltpu.VMEM((2, pairs, 2 * state, LANES), BF16),
            pltpu.VMEM((2, *unit), BF16),
            pltpu.VMEM(inputs.shape, BF16),
            pltpu.VMEM(step_sizes.shape, F32),
            pltpu.VMEM(input_map.shape, BF16),
            pltpu.VMEM(output_map.shape, BF16),
            pltpu.VMEM((1, tokens), jnp.int32),
            pltpu.VMEM(cotangent.shape, BF16),
            dma((6,)),
        ],
        compiler_params=pltpu.CompilerParams(
            collective_id=0, has_side_effects=True, vmem_limit_bytes=48 << 20
        ),
    )(
        inputs, step_sizes, input_map, output_map, level_table,
        token_class.reshape(1, tokens), cotangent,
    )
    return pl.pallas_call(
        write_out,
        out_shape=tuple(jax.ShapeDtypeStruct(r.shape, r.dtype) for r in results),
        in_specs=[vmem] * 6,
        out_specs=(hbm,) * 6,
        scratch_shapes=[dma((6,))],
        compiler_params=pltpu.CompilerParams(vmem_limit_bytes=8 << 20),
    )(*results)


def solution(mesh):
    placed = (
        P("seq", "head"),
        P("head", "seq"),
        P("seq", None),
        P("seq", None),
        P("head", None, None),
        P("seq"),
        P("seq", "head"),
    )
    return jax.shard_map(
        local,
        mesh=mesh,
        in_specs=placed,
        out_specs=(
            P("seq", "head"),
            P("seq", "head"),
            P("head", "seq"),
            P("seq", None),
            P("seq", None),
            P("head", None, None),
        ),
        check_vma=False,
    )
```

```python
import functools
import math

import jax
import jax.numpy as jnp
from jax import lax
from jax.experimental import pallas as pl
from jax.experimental.pallas import tpu as pltpu
from jax.sharding import PartitionSpec as P

Q = 128
LANES = 128
F32 = jnp.float32
BF16 = jnp.bfloat16
HIGH = lax.Precision.HIGHEST
MESH = pl.DeviceIdType.MESH


def dot(a, b, ca, cb, precision=None):
    return lax.dot_general(
        a, b, (((ca,), (cb,)), ((), ())), precision=precision, preferred_element_type=F32
    )


def scale_of(level):
    return 1.0 if level == 0 else 2.0 ** (-(level - 1) / 2)


def kernel(
    dims,
    x_hbm,
    step_hbm,
    bin_hbm,
    cout_hbm,
    table_hbm,
    class_hbm,
    g_hbm,
    out_ref,
    xg_ref,
    sg_ref,
    ing_ref,
    outg_ref,
    tg_ref,
    stepx,
    scaled,
    clsb,
    lev,
    scores,
    mo2,
    s0,
    q1,
    qown,
    frun,
    rrun,
    fcs,
    fsrc,
    nout,
    nback,
    score_sum,
    in_acc,
    out_acc,
    tab,
    send_f,
    recv_f,
    send_r,
    recv_r,
    part_send,
    part_recv,
    part_own,
    final,
    tsend,
    trecv,
    f_ssem,
    f_rsem,
    r_ssem,
    r_rsem,
    p_ssem,
    p_rsem,
    a_ssem,
    a_rsem,
    t_ssem,
    t_rsem,
    steprow,
    sgrow,
    class_b,
    source_b,
    x_ref,
    step_ref,
    bin_ref,
    cout_ref,
    class_ref,
    g_ref,
    table_ref,
    in_sem,
):
    heads, width, tokens, state, levels, nb, n_head, total = dims
    per = LANES // width
    pairs = heads // per
    sb = Q.bit_length() - 1
    mid = sb + 1
    far0 = mid + 1
    device = lax.axis_index("seq")
    mine = lax.axis_index("head")

    barrier = pltpu.get_barrier_semaphore()
    for i in range(1, 1 << nb):
        pl.semaphore_signal(barrier, inc=1, device_id={"seq": device ^ i}, device_id_type=MESH)
    for i in range(1, n_head):
        pl.semaphore_signal(
            barrier, inc=1, device_id={"head": lax.rem(mine + i, n_head)}, device_id_type=MESH
        )

    loads = [
        pltpu.make_async_copy(src, dst, in_sem.at[i])
        for i, (src, dst) in enumerate(
            [
                (class_hbm, class_ref),
                (cout_hbm, cout_ref),
                (bin_hbm, bin_ref),
                (step_hbm, step_ref),
                (x_hbm, x_ref),
                (g_hbm, g_ref),
                (table_hbm, table_ref),
            ]
        )
    ]
    for load in loads:
        load.start()

    lane = lax.broadcasted_iota(jnp.int32, (1, LANES), 1)
    halves = [(lane // width == j) for j in range(per)]
    half_f = [m.astype(F32) for m in halves]
    half_b = [m.astype(F32).astype(BF16) for m in halves]
    zero = jnp.zeros((state, LANES), F32)

    def wrow(p, k, level):
        row = jnp.zeros((1, LANES), F32)
        for j in range(per):
            row = jnp.where(halves[j], table_ref[p * per + j, k, level] * scale_of(level), row)
        return row

    def cols(p):
        return pl.ds(pl.multiple_of(p * LANES, LANES), LANES)

    for load in loads:
        load.wait()
    row = class_ref[...].astype(F32)
    clsb[...] = dot(
        jnp.broadcast_to(row, (16, tokens)).astype(BF16),
        jnp.full((16, LANES), 0.0625, BF16),
        0,
        0,
    )
    t_id = lax.broadcasted_iota(jnp.int32, (Q, Q), 0)
    s_id = lax.broadcasted_iota(jnp.int32, (Q, Q), 1)
    differ = t_id ^ s_id
    level_id = jnp.zeros((Q, Q), jnp.int32)
    for bit in range(sb):
        level_id = level_id + (differ >= (1 << bit)).astype(jnp.int32)
    lev[...] = jnp.where(t_id >= s_id, level_id, -1)
    spans = [slice(c * Q, (c + 1) * Q) for c in range(2)]
    for c in range(2):
        scores[c] = dot(cout_ref[spans[c], :], bin_ref[spans[c], :], 1, 1)
        one = clsb[spans[c], :]
        mo = cout_ref[spans[c], :].astype(F32)
        mo2[c, :, :state] = (mo * (1.0 - one)).astype(BF16)
        mo2[c, :, state:] = (mo * one).astype(BF16)
    for h in range(heads):
        for c in range(2):
            steprow[h, c : c + 1, :] = step_ref[h : h + 1, spans[c]]
    score_sum[...] = jnp.zeros_like(score_sum)
    in_acc[...] = jnp.zeros_like(in_acc)
    out_acc[...] = jnp.zeros_like(out_acc)
    tab[...] = jnp.zeros_like(tab)

    def f_copy(b, p):
        return pltpu.make_async_remote_copy(
            send_f.at[b, p], recv_f.at[b, p], f_ssem.at[b, p], f_rsem.at[b, p],
            device_id={"seq": device ^ (1 << b)}, device_id_type=MESH,
        )

    def r_copy(b, k, p):
        return pltpu.make_async_remote_copy(
            send_r.at[b, k, p], recv_r.at[b, k, p], r_ssem.at[b, k, p], r_rsem.at[b, k, p],
            device_id={"seq": device ^ (1 << b)}, device_id_type=MESH,
        )

    bit_of = [(device >> b) & 1 for b in range(nb)]
    above = [device >> (b + 1) for b in range(nb)]
    ones = [(1 << (nb - b - 1)) - 1 for b in range(nb)]
    f_sent = [(bit_of[b] == 0) | (above[b] != ones[b]) for b in range(nb)]
    f_came = [(bit_of[b] == 1) | (above[b] != ones[b]) for b in range(nb)]
    count = [sum(bit_of[b + 1 :], jnp.int32(0)) for b in range(nb)]
    c_sent = [(bit_of[b] == 1) & (count[b] <= 1) for b in range(nb)]
    c_came = [(bit_of[b] == 0) & (count[b] <= 1) for b in range(nb)]
    r_none = [count[b] == 0 for b in range(nb)]
    r_one = [count[b] == 1 for b in range(nb)]
    r_both = [count[b] >= 2 for b in range(nb)]

    def combined(p, level_row):
        return level_row(0) * rrun[0, p] + level_row(1) * rrun[1, p]

    def start(b, p):
        @pl.when(f_sent[b])
        def _():
            send_f[b, p] = frun[p].astype(BF16)
            f_copy(b, p).start()

        @pl.when(c_sent[b])
        def _():
            def now():
                return combined(p, lambda k: wrow(p, k, far0 + b)).astype(BF16)

            if b == 0:
                send_r[b, 0, p] = now()
            else:

                @pl.when(r_one[b])
                def _():
                    send_r[b, 0, p] = now()

                @pl.when(r_none[b])
                def _():
                    send_r[b, 0, p] = rrun[0, p].astype(BF16)

            r_copy(b, 0, p).start()

        @pl.when(r_one[b])
        def _():
            def later(k):
                row = wrow(p, k, far0 + nb - 1)
                for other in range(b + 1, nb - 1):
                    row = jnp.where(bit_of[other] == 1, wrow(p, k, far0 + other), row)
                return row

            if b == 0:
                rrun[0, p] = combined(p, later)
            else:

                @pl.when(bit_of[b] == 1)
                def _():
                    rrun[0, p] = combined(p, later)

            send_r[b, 1, p] = rrun[0, p].astype(BF16)
            r_copy(b, 1, p).start()

        @pl.when(r_both[b])
        def _():
            for k in range(2):
                send_r[b, k, p] = rrun[k, p].astype(BF16)
                r_copy(b, k, p).start()

    def put_rows(k, level, p, value):
        for j in range(per):
            tab[k * levels + level, pl.ds(p * per + j, 1), :] = value * half_f[j]

    def combine(b, p):
        @pl.when(f_came[b])
        def _():
            f_copy(b, p).wait_recv()
            got = recv_f[b, p].astype(F32)
            frun[p] = frun[p] + got

        @pl.when(bit_of[b] == 1)
        def _():
            got = recv_f[b, p].astype(F32)
            for k in range(2):
                fcs[k, p] = fcs[k, p] + wrow(p, k, far0 + b) * got
                put_rows(k, far0 + b, p, jnp.sum(got * qown[k, p], axis=0, keepdims=True))

        @pl.when(c_came[b])
        def _():
            r_copy(b, 0, p).wait_recv()
            fsrc[p] = fsrc[p] + recv_r[b, 0, p].astype(F32)

        @pl.when(r_one[b])
        def _():
            r_copy(b, 1, p).wait_recv()
            rrun[0, p] = rrun[0, p] + recv_r[b, 1, p].astype(F32)

        @pl.when(r_both[b])
        def _():
            for k in range(2):
                r_copy(b, k, p).wait_recv()
                got = recv_r[b, k, p].astype(F32)
                rrun[k, p] = rrun[k, p] + got

            @pl.when(bit_of[b] == 0)
            def _():
                fsrc[p] = (
                    fsrc[p]
                    + wrow(p, 0, far0 + b) * recv_r[b, 0, p].astype(F32)
                    + wrow(p, 1, far0 + b) * recv_r[b, 1, p].astype(F32)
                )

    def states(p, carry):
        picks = (
            lax.broadcasted_iota(jnp.int32, (heads, LANES), 0)
            == p * per + lax.broadcasted_iota(jnp.int32, (heads, LANES), 1) // width
        ).astype(F32)
        grown = dot(step_ref[...], picks, 0, 0, HIGH)
        stepx[p] = grown
        sc = (x_ref[:, cols(p)].astype(F32) * grown).astype(BF16)
        scaled[p] = sc
        st = [dot(bin_ref[spans[c], :], sc[spans[c]], 0, 0) for c in range(2)]
        s0[p] = st[0]
        frun[p] = st[0] + st[1]
        q = [dot(mo2[c], g_ref[spans[c], cols(p)], 0, 0) for c in range(2)]
        for k in range(2):
            part = [q[c][k * state : (k + 1) * state] for c in range(2)]
            q1[k, p] = part[1]
            both = part[0] + part[1]
            qown[k, p] = both
            rrun[k, p] = both
            fcs[k, p] = zero
            put_rows(k, mid, p, jnp.sum(st[0] * part[1], axis=0, keepdims=True))
        fsrc[p] = zero
        return carry

    def begin(p, carry):
        start(0, p)
        return carry

    def states_begin(p, carry):
        states(p, carry)
        return begin(p, carry)

    pl.semaphore_wait(barrier, (1 << nb) - 1 + n_head - 1)
    lax.fori_loop(0, pairs, states_begin, 0)

    def near(p, carry):
        lv = lev[...]
        hit = [lv == level for level in range(sb + 1)]
        weights = []
        for j in range(per):
            rows = []
            for k in range(2):
                acc = jnp.zeros((Q, Q), F32)
                for level in range(sb + 1):
                    acc = jnp.where(
                        hit[level], table_ref[p * per + j, k, level] * scale_of(level), acc
                    )
                rows.append(acc)
            weights.append(rows)
        terms = [[jnp.zeros((Q, Q), F32) for k in range(2)] for j in range(per)]
        for c in range(2):
            x = x_ref[spans[c], cols(p)]
            g = g_ref[spans[c], cols(p)]
            xs = jnp.concatenate([x * half_b[j] for j in range(per)], axis=0)
            gs = jnp.concatenate([g * half_b[j] for j in range(per)], axis=0)
            mg = dot(gs, x, 1, 1)
            is_one = clsb[spans[c], :] > 0.5
            score = scores[c]
            mixes = []
            total_sg = score_sum[c]
            for j in range(per):
                head = p * per + j
                step = steprow[head, c : c + 1, :]
                weight = jnp.where(is_one, weights[j][1], weights[j][0])
                ws = weight * step
                mgj = mg[j * Q : (j + 1) * Q]
                mixes.append((score * ws).astype(BF16))
                total_sg = total_sg + mgj * ws
                graded = mgj * score
                sgrow[head, c : c + 1, :] = jnp.sum(graded * weight, axis=0, keepdims=True)
                term = graded * step
                terms[j][0] = terms[j][0] + jnp.where(is_one, 0.0, term)
                terms[j][1] = terms[j][1] + jnp.where(is_one, term, 0.0)
            score_sum[c] = total_sg
            nout[p, spans[c], :] = dot(jnp.concatenate(mixes, axis=1), xs, 1, 0)
            nback[p, spans[c], :] = dot(jnp.concatenate(mixes, axis=0), gs, 0, 0)
        for j in range(per):
            for k in range(2):
                term = terms[j][k]
                for level in range(sb + 1):
                    if level <= 3:
                        value = jnp.sum(jnp.where(hit[level], term, 0.0), axis=0, keepdims=True)
                    else:
                        size = 1 << (level - 1)
                        value = jnp.zeros((1, LANES), F32)
                        for odd in range(1, Q // size, 2):
                            rows = jnp.sum(term[odd * size : (odd + 1) * size], axis=0, keepdims=True)
                            value = jnp.where(lane // size == odd - 1, rows, value)
                    tab[k * levels + level, pl.ds(p * per + j, 1), :] = value
        return carry

    def far_maps(p):
        for c in range(2):
            cs = []
            for k in range(2):
                value = fcs[k, p]
                if c == 1:
                    value = value + wrow(p, k, mid) * s0[p]
                cs.append(value.astype(BF16))
            cs = jnp.concatenate(cs, axis=0)
            src = fsrc[p]
            if c == 0:
                src = src + wrow(p, 0, mid) * q1[0, p] + wrow(p, 1, mid) * q1[1, p]
            src = src.astype(BF16)
            class_b[c, p] = cs
            source_b[c, p] = src
            in_acc[c] = in_acc[c] + dot(scaled[p, spans[c], :], src, 1, 1)
            out_acc[c] = out_acc[c] + dot(g_ref[spans[c], cols(p)], cs, 1, 1)

    def far_values(p):
        for c in range(2):
            cs = class_b[c, p]
            src = source_b[c, p]
            read = dot(mo2[c], cs, 1, 0)
            out_ref[spans[c], cols(p)] = (nout[p, spans[c], :] + read).astype(BF16)
            vg = dot(bin_ref[spans[c], :], src, 1, 0)
            xg_ref[spans[c], cols(p)] = (
                nback[p, spans[c], :] + stepx[p, spans[c], :] * vg
            ).astype(BF16)
            picks = jnp.concatenate(half_f + [jnp.zeros((8 - per, LANES), F32)], axis=0)
            far_step = dot(picks, x_ref[spans[c], cols(p)].astype(F32) * vg, 1, 1, HIGH)
            for j in range(per):
                at = (p * per + j, slice(c, c + 1), slice(None))
                sgrow[at] = sgrow[at] + far_step[j : j + 1]

    lag = 2

    def pipeline(i, carry):
        last = i - lag * (nb - 1)

        @pl.when(last > 0)
        def _():
            far_values(last - 1)

        @pl.when(i < pairs)
        def _():
            near(i, 0)

        for b in range(nb):
            p = i - lag * b

            @pl.when((p >= 0) & (p < pairs))
            def _(b=b, p=p):
                combine(b, p)
                if b + 1 < nb:
                    start(b + 1, p)
                else:
                    far_maps(p)

        return carry

    lax.fori_loop(0, pairs + lag * (nb - 1), pipeline, 0)

    grads = [[], []]
    for c in range(2):
        sgb = score_sum[c].astype(BF16)
        is_one = clsb[spans[c], :] > 0.5
        acc = out_acc[c]
        grads[0].append(in_acc[c] + dot(sgb, cout_ref[spans[c], :], 0, 0))
        grads[1].append(
            jnp.where(is_one, acc[:, state:], acc[:, :state])
            + dot(sgb, bin_ref[spans[c], :], 1, 0)
        )
    full = jnp.concatenate(grads[0] + grads[1], axis=0)
    rows = 2 * tokens // n_head
    for q in range(n_head):
        part_own[q] = full[q * rows : (q + 1) * rows]
        part_send[q] = full[q * rows : (q + 1) * rows].astype(BF16)

    def part_copy(i):
        to = lax.rem(mine + i, n_head)
        return pltpu.make_async_remote_copy(
            part_send.at[to], part_recv.at[i], p_ssem.at[i], p_rsem.at[i],
            device_id={"head": to}, device_id_type=MESH,
        )

    def all_copy(i, slot):
        to = lax.rem(mine + i, n_head)
        return pltpu.make_async_remote_copy(
            final.at[slot], final.at[slot], a_ssem.at[i], a_rsem.at[i],
            device_id={"head": to}, device_id_type=MESH,
        )

    for i in range(1, n_head):
        part_copy(i).start()
    def table_copy(i):
        return pltpu.make_async_remote_copy(
            tsend, trecv.at[i], t_ssem.at[i], t_rsem.at[i],
            device_id={"seq": device ^ i}, device_id_type=MESH,
        )

    table_sum = []
    for k in range(2):
        acc = jnp.zeros((heads, LANES), F32)
        for level in range(levels):
            col = jnp.sum(tab[k * levels + level], axis=1, keepdims=True)
            acc = jnp.where(lane == level, col * (scale_of(level) / math.sqrt(total)), acc)
        table_sum.append(acc)
    for k in range(2):
        tsend[k, :heads, :] = table_sum[k]
        trecv[0, k, :heads, :] = table_sum[k]
    for i in range(1, 1 << nb):
        table_copy(i).start()

    far_values(pairs - 1)
    for h in range(heads):
        for c in range(2):
            sg_ref[h : h + 1, spans[c]] = sgrow[h, c : c + 1, :]
    summed = part_own[mine]
    for i in range(1, n_head):
        part_copy(i).wait_recv()
        summed = summed + part_recv[i].astype(F32)
    final[mine] = summed.astype(BF16)
    for i in range(1, n_head):
        all_copy(i, mine).start()
    for i in range(1, 1 << nb):
        table_copy(i).wait_recv()
    for k in range(2):
        table_sum[k] = trecv[device, k, :heads, :]
        for owner in range(1, 1 << nb):
            table_sum[k] = table_sum[k] + trecv[device ^ owner, k, :heads, :]
    for k in range(2):
        tg_ref[:, k, :] = table_sum[k][:, :levels]
    for i in range(1, n_head):
        all_copy(i, lax.rem(mine + n_head - i, n_head)).wait_recv()
    per_out = n_head // 2
    for q in range(n_head):
        where = (slice((q % per_out) * rows, (q % per_out + 1) * rows), slice(None))
        (ing_ref if q < per_out else outg_ref)[where] = final[q].astype(F32)

    for i in range(1, n_head):
        part_copy(i).wait_send()
        all_copy(i, mine).wait_send()
    for i in range(1, 1 << nb):
        table_copy(i).wait_send()
    for b in range(nb):

        def drain(p, carry, b=b):
            @pl.when(f_sent[b])
            def _():
                f_copy(b, p).wait_send()

            @pl.when(c_sent[b])
            def _():
                r_copy(b, 0, p).wait_send()

            @pl.when(r_one[b])
            def _():
                r_copy(b, 1, p).wait_send()

            @pl.when(r_both[b])
            def _():
                for k in range(2):
                    r_copy(b, k, p).wait_send()

            return carry

        lax.fori_loop(0, pairs, drain, 0)


def write_out(*refs):
    sem = refs[-1]
    copies = [pltpu.make_async_copy(refs[i], refs[6 + i], sem.at[i]) for i in range(6)]
    for copy in copies:
        copy.start()
    for copy in copies:
        copy.wait()


def local(inputs, step_sizes, input_map, output_map, level_table, token_class, cotangent):
    tokens, state = input_map.shape
    heads = step_sizes.shape[0]
    width = inputs.shape[1] // heads
    levels = level_table.shape[2]
    n_seq = lax.axis_size("seq")
    n_head = lax.axis_size("head")
    nb = n_seq.bit_length() - 1
    per = LANES // width
    pairs = heads // per
    assert tokens == 2 * Q and heads % per == 0 and n_head % 2 == 0 and nb > 0
    assert level_table.shape[1] == 2 and state == Q
    dims = (heads, width, tokens, state, levels, nb, n_head, float(tokens * n_seq))
    rows = 2 * tokens // n_head
    vmem = pl.BlockSpec(memory_space=pltpu.VMEM)
    hbm = pl.BlockSpec(memory_space=pltpu.HBM)
    dma = pltpu.SemaphoreType.DMA
    unit = (pairs, state, LANES)
    tall = (pairs, tokens, LANES)
    padded = -(-heads // 8) * 8
    placed = [
        pltpu.with_memory_space_constraint(a, pltpu.HBM)
        for a in (
            inputs, step_sizes, input_map, output_map, level_table,
            token_class.reshape(1, tokens), cotangent,
        )
    ]
    results = pl.pallas_call(
        functools.partial(kernel, dims),
        out_shape=(
            jax.ShapeDtypeStruct(inputs.shape, BF16),
            jax.ShapeDtypeStruct(inputs.shape, BF16),
            jax.ShapeDtypeStruct(step_sizes.shape, F32),
            jax.ShapeDtypeStruct(input_map.shape, F32),
            jax.ShapeDtypeStruct(output_map.shape, F32),
            jax.ShapeDtypeStruct(level_table.shape, F32),
        ),
        in_specs=[hbm] * 7,
        out_specs=(vmem,) * 6,
        scratch_shapes=[
            pltpu.VMEM(tall, F32),
            pltpu.VMEM(tall, BF16),
            pltpu.VMEM((tokens, LANES), F32),
            pltpu.VMEM((Q, Q), jnp.int32),
            pltpu.VMEM((2, Q, Q), F32),
            pltpu.VMEM((2, Q, 2 * state), BF16),
            pltpu.VMEM(unit, F32),
            pltpu.VMEM((2, *unit), F32),
            pltpu.VMEM((2, *unit), F32),
            pltpu.VMEM(unit, F32),
            pltpu.VMEM((2, *unit), F32),
            pltpu.VMEM((2, *unit), F32),
            pltpu.VMEM(unit, F32),
            pltpu.VMEM(tall, F32),
            pltpu.VMEM(tall, F32),
            pltpu.VMEM((2, Q, Q), F32),
            pltpu.VMEM((2, Q, state), F32),
            pltpu.VMEM((2, Q, 2 * state), F32),
            pltpu.VMEM((2 * levels, heads, LANES), F32),
            pltpu.VMEM((nb, *unit), BF16),
            pltpu.VMEM((nb, *unit), BF16),
            pltpu.VMEM((nb, 2, *unit), BF16),
            pltpu.VMEM((nb, 2, *unit), BF16),
            pltpu.VMEM((n_head, rows, state), BF16),
            pltpu.VMEM((n_head, rows, state), BF16),
            pltpu.VMEM((n_head, rows, state), F32),
            pltpu.VMEM((n_head, rows, state), BF16),
            pltpu.VMEM((2, padded, LANES), F32),
            pltpu.VMEM((n_seq, 2, padded, LANES), F32),
            dma((nb, pairs)),
            dma((nb, pairs)),
            dma((nb, 2, pairs)),
            dma((nb, 2, pairs)),
            dma((n_head,)),
            dma((n_head,)),
            dma((n_head,)),
            dma((n_head,)),
            dma((n_seq,)),
            dma((n_seq,)),
            pltpu.VMEM((heads, 2, LANES), F32),
            pltpu.VMEM((heads, 2, LANES), F32),
            pltpu.VMEM((2, pairs, 2 * state, LANES), BF16),
            pltpu.VMEM((2, *unit), BF16),
            pltpu.VMEM(inputs.shape, BF16),
            pltpu.VMEM(step_sizes.shape, F32),
            pltpu.VMEM(input_map.shape, BF16),
            pltpu.VMEM(output_map.shape, BF16),
            pltpu.VMEM((1, tokens), jnp.int32),
            pltpu.VMEM(cotangent.shape, BF16),
            pltpu.SMEM(level_table.shape, F32),
            dma((7,)),
        ],
        compiler_params=pltpu.CompilerParams(
            collective_id=0, has_side_effects=True, vmem_limit_bytes=48 << 20
        ),
    )(*placed)
    return pl.pallas_call(
        write_out,
        out_shape=tuple(jax.ShapeDtypeStruct(r.shape, r.dtype) for r in results),
        in_specs=[vmem] * 6,
        out_specs=(hbm,) * 6,
        scratch_shapes=[dma((6,))],
        compiler_params=pltpu.CompilerParams(vmem_limit_bytes=8 << 20),
    )(*results)


def solution(mesh):
    placed = (
        P("seq", "head"),
        P("head", "seq"),
        P("seq", None),
        P("seq", None),
        P("head", None, None),
        P("seq"),
        P("seq", "head"),
    )
    return jax.shard_map(
        local,
        mesh=mesh,
        in_specs=placed,
        out_specs=(
            P("seq", "head"),
            P("seq", "head"),
            P("head", "seq"),
            P("seq", None),
            P("seq", None),
            P("head", None, None),
        ),
        check_vma=False,
    )
```

```python
import functools
import math

import jax
import jax.numpy as jnp
from jax import lax
from jax.experimental import pallas as pl
from jax.experimental.pallas import tpu as pltpu
from jax.sharding import PartitionSpec as P

Q = 128
LANES = 128
F32 = jnp.float32
BF16 = jnp.bfloat16
HIGH = lax.Precision.HIGHEST
MESH = pl.DeviceIdType.MESH


def dot(a, b, ca, cb, precision=None):
    return lax.dot_general(
        a, b, (((ca,), (cb,)), ((), ())), precision=precision, preferred_element_type=F32
    )


def scale_of(level):
    return 1.0 if level == 0 else 2.0 ** (-(level - 1) / 2)


def kernel(
    dims,
    x_hbm,
    step_hbm,
    bin_hbm,
    cout_hbm,
    table_hbm,
    class_hbm,
    g_hbm,
    out_ref,
    xg_ref,
    sg_ref,
    ing_ref,
    outg_ref,
    tg_ref,
    stepx,
    scaled,
    clsb,
    lev,
    scores,
    mo2,
    s0,
    q1,
    qown,
    frun,
    rrun,
    fcs,
    fsrc,
    nout,
    nback,
    score_sum,
    in_acc,
    out_acc,
    tab,
    send_f,
    recv_f,
    send_r,
    recv_r,
    part_send,
    part_recv,
    part_own,
    final,
    tsend,
    trecv,
    f_ssem,
    f_rsem,
    r_ssem,
    r_rsem,
    p_ssem,
    p_rsem,
    a_ssem,
    a_rsem,
    t_ssem,
    t_rsem,
    steprow,
    sgrow,
    class_b,
    source_b,
    x_ref,
    step_ref,
    bin_ref,
    cout_ref,
    class_ref,
    g_ref,
    table_ref,
    in_sem,
):
    heads, width, tokens, state, levels, nb, n_head, total = dims
    per = LANES // width
    pairs = heads // per
    sb = Q.bit_length() - 1
    mid = sb + 1
    far0 = mid + 1
    device = lax.axis_index("seq")
    mine = lax.axis_index("head")

    barrier = pltpu.get_barrier_semaphore()
    for i in range(1, 1 << nb):
        pl.semaphore_signal(barrier, inc=1, device_id={"seq": device ^ i}, device_id_type=MESH)
    for i in range(1, n_head):
        pl.semaphore_signal(
            barrier, inc=1, device_id={"head": lax.rem(mine + i, n_head)}, device_id_type=MESH
        )

    loads = [
        pltpu.make_async_copy(src, dst, in_sem.at[i])
        for i, (src, dst) in enumerate(
            [
                (class_hbm, class_ref),
                (cout_hbm, cout_ref),
                (bin_hbm, bin_ref),
                (step_hbm, step_ref),
                (x_hbm, x_ref),
                (g_hbm, g_ref),
                (table_hbm, table_ref),
            ]
        )
    ]
    for load in loads:
        load.start()

    lane = lax.broadcasted_iota(jnp.int32, (1, LANES), 1)
    halves = [(lane // width == j) for j in range(per)]
    half_f = [m.astype(F32) for m in halves]
    half_b = [m.astype(F32).astype(BF16) for m in halves]
    zero = jnp.zeros((state, LANES), F32)

    def wrow(p, k, level):
        row = jnp.zeros((1, LANES), F32)
        for j in range(per):
            row = jnp.where(halves[j], table_ref[p * per + j, k, level] * scale_of(level), row)
        return row

    def cols(p):
        return pl.ds(pl.multiple_of(p * LANES, LANES), LANES)

    for load in loads[:4]:
        load.wait()
    row = class_ref[...].astype(F32)
    clsb[...] = dot(
        jnp.broadcast_to(row, (16, tokens)).astype(BF16),
        jnp.full((16, LANES), 0.0625, BF16),
        0,
        0,
    )
    t_id = lax.broadcasted_iota(jnp.int32, (Q, Q), 0)
    s_id = lax.broadcasted_iota(jnp.int32, (Q, Q), 1)
    differ = t_id ^ s_id
    level_id = jnp.zeros((Q, Q), jnp.int32)
    for bit in range(sb):
        level_id = level_id + (differ >= (1 << bit)).astype(jnp.int32)
    lev[...] = jnp.where(t_id >= s_id, level_id, -1)
    spans = [slice(c * Q, (c + 1) * Q) for c in range(2)]
    for c in range(2):
        scores[c] = dot(cout_ref[spans[c], :], bin_ref[spans[c], :], 1, 1)
        one = clsb[spans[c], :]
        mo = cout_ref[spans[c], :].astype(F32)
        mo2[c, :, :state] = (mo * (1.0 - one)).astype(BF16)
        mo2[c, :, state:] = (mo * one).astype(BF16)
    for h in range(heads):
        for c in range(2):
            steprow[h, c : c + 1, :] = step_ref[h : h + 1, spans[c]]
    score_sum[...] = jnp.zeros_like(score_sum)
    in_acc[...] = jnp.zeros_like(in_acc)
    out_acc[...] = jnp.zeros_like(out_acc)
    tab[...] = jnp.zeros_like(tab)

    def f_copy(b, p):
        return pltpu.make_async_remote_copy(
            send_f.at[b, p], recv_f.at[b, p], f_ssem.at[b, p], f_rsem.at[b, p],
            device_id={"seq": device ^ (1 << b)}, device_id_type=MESH,
        )

    def r_copy(b, k, p):
        return pltpu.make_async_remote_copy(
            send_r.at[b, k, p], recv_r.at[b, k, p], r_ssem.at[b, k, p], r_rsem.at[b, k, p],
            device_id={"seq": device ^ (1 << b)}, device_id_type=MESH,
        )

    bit_of = [(device >> b) & 1 for b in range(nb)]
    above = [device >> (b + 1) for b in range(nb)]
    ones = [(1 << (nb - b - 1)) - 1 for b in range(nb)]
    f_sent = [(bit_of[b] == 0) | (above[b] != ones[b]) for b in range(nb)]
    f_came = [(bit_of[b] == 1) | (above[b] != ones[b]) for b in range(nb)]
    count = [sum(bit_of[b + 1 :], jnp.int32(0)) for b in range(nb)]
    c_sent = [(bit_of[b] == 1) & (count[b] <= 1) for b in range(nb)]
    c_came = [(bit_of[b] == 0) & (count[b] <= 1) for b in range(nb)]
    r_none = [count[b] == 0 for b in range(nb)]
    r_one = [count[b] == 1 for b in range(nb)]
    r_both = [count[b] >= 2 for b in range(nb)]

    def combined(p, level_row):
        return level_row(0) * rrun[0, p] + level_row(1) * rrun[1, p]

    def start(b, p):
        @pl.when(f_sent[b])
        def _():
            send_f[b, p] = frun[p].astype(BF16)
            f_copy(b, p).start()

        @pl.when(c_sent[b])
        def _():
            def now():
                return combined(p, lambda k: wrow(p, k, far0 + b)).astype(BF16)

            if b == 0:
                send_r[b, 0, p] = now()
            else:

                @pl.when(r_one[b])
                def _():
                    send_r[b, 0, p] = now()

                @pl.when(r_none[b])
                def _():
                    send_r[b, 0, p] = rrun[0, p].astype(BF16)

            r_copy(b, 0, p).start()

        @pl.when(r_one[b])
        def _():
            def later(k):
                row = wrow(p, k, far0 + nb - 1)
                for other in range(b + 1, nb - 1):
                    row = jnp.where(bit_of[other] == 1, wrow(p, k, far0 + other), row)
                return row

            if b == 0:
                rrun[0, p] = combined(p, later)
            else:

                @pl.when(bit_of[b] == 1)
                def _():
                    rrun[0, p] = combined(p, later)

            send_r[b, 1, p] = rrun[0, p].astype(BF16)
            r_copy(b, 1, p).start()

        @pl.when(r_both[b])
        def _():
            for k in range(2):
                send_r[b, k, p] = rrun[k, p].astype(BF16)
                r_copy(b, k, p).start()

    def put_rows(k, level, p, value):
        for j in range(per):
            tab[k * levels + level, pl.ds(p * per + j, 1), :] = value * half_f[j]

    def combine(b, p):
        @pl.when(f_came[b])
        def _():
            f_copy(b, p).wait_recv()
            got = recv_f[b, p].astype(F32)
            frun[p] = frun[p] + got

        @pl.when(bit_of[b] == 1)
        def _():
            got = recv_f[b, p].astype(F32)
            for k in range(2):
                fcs[k, p] = fcs[k, p] + wrow(p, k, far0 + b) * got
                put_rows(k, far0 + b, p, jnp.sum(got * qown[k, p], axis=0, keepdims=True))

        @pl.when(c_came[b])
        def _():
            r_copy(b, 0, p).wait_recv()
            fsrc[p] = fsrc[p] + recv_r[b, 0, p].astype(F32)

        @pl.when(r_one[b])
        def _():
            r_copy(b, 1, p).wait_recv()
            rrun[0, p] = rrun[0, p] + recv_r[b, 1, p].astype(F32)

        @pl.when(r_both[b])
        def _():
            for k in range(2):
                r_copy(b, k, p).wait_recv()
                got = recv_r[b, k, p].astype(F32)
                rrun[k, p] = rrun[k, p] + got

            @pl.when(bit_of[b] == 0)
            def _():
                fsrc[p] = (
                    fsrc[p]
                    + wrow(p, 0, far0 + b) * recv_r[b, 0, p].astype(F32)
                    + wrow(p, 1, far0 + b) * recv_r[b, 1, p].astype(F32)
                )

    def states(p, carry):
        picks = (
            lax.broadcasted_iota(jnp.int32, (heads, LANES), 0)
            == p * per + lax.broadcasted_iota(jnp.int32, (heads, LANES), 1) // width
        ).astype(F32)
        grown = dot(step_ref[...], picks, 0, 0, HIGH)
        stepx[p] = grown
        sc = (x_ref[:, cols(p)].astype(F32) * grown).astype(BF16)
        scaled[p] = sc
        st = [dot(bin_ref[spans[c], :], sc[spans[c]], 0, 0) for c in range(2)]
        s0[p] = st[0]
        frun[p] = st[0] + st[1]
        q = [dot(mo2[c], g_ref[spans[c], cols(p)], 0, 0) for c in range(2)]
        for k in range(2):
            part = [q[c][k * state : (k + 1) * state] for c in range(2)]
            q1[k, p] = part[1]
            both = part[0] + part[1]
            qown[k, p] = both
            rrun[k, p] = both
            fcs[k, p] = zero
            put_rows(k, mid, p, jnp.sum(st[0] * part[1], axis=0, keepdims=True))
        fsrc[p] = zero
        return carry

    def begin(p, carry):
        start(0, p)
        return carry

    def states_begin(p, carry):
        states(p, carry)
        return begin(p, carry)

    for load in loads[4:]:
        load.wait()
    pl.semaphore_wait(barrier, (1 << nb) - 1 + n_head - 1)
    lax.fori_loop(0, pairs, states_begin, 0)

    def near(p, carry):
        lv = lev[...]
        hit = [lv == level for level in range(sb + 1)]
        weights = []
        for j in range(per):
            rows = []
            for k in range(2):
                acc = jnp.zeros((Q, Q), F32)
                for level in range(sb + 1):
                    acc = jnp.where(
                        hit[level], table_ref[p * per + j, k, level] * scale_of(level), acc
                    )
                rows.append(acc)
            weights.append(rows)
        terms = [[jnp.zeros((Q, Q), F32) for k in range(2)] for j in range(per)]
        for c in range(2):
            x = x_ref[spans[c], cols(p)]
            g = g_ref[spans[c], cols(p)]
            xs = jnp.concatenate([x * half_b[j] for j in range(per)], axis=0)
            gs = jnp.concatenate([g * half_b[j] for j in range(per)], axis=0)
            mg = dot(gs, x, 1, 1)
            is_one = clsb[spans[c], :] > 0.5
            score = scores[c]
            mixes = []
            total_sg = score_sum[c]
            for j in range(per):
                head = p * per + j
                step = steprow[head, c : c + 1, :]
                weight = jnp.where(is_one, weights[j][1], weights[j][0])
                ws = weight * step
                mgj = mg[j * Q : (j + 1) * Q]
                mixes.append((score * ws).astype(BF16))
                total_sg = total_sg + mgj * ws
                graded = mgj * score
                sgrow[head, c : c + 1, :] = jnp.sum(graded * weight, axis=0, keepdims=True)
                term = graded * step
                terms[j][0] = terms[j][0] + jnp.where(is_one, 0.0, term)
                terms[j][1] = terms[j][1] + jnp.where(is_one, term, 0.0)
            score_sum[c] = total_sg
            nout[p, spans[c], :] = dot(jnp.concatenate(mixes, axis=1), xs, 1, 0)
            nback[p, spans[c], :] = dot(jnp.concatenate(mixes, axis=0), gs, 0, 0)
        for j in range(per):
            for k in range(2):
                term = terms[j][k]
                for level in range(sb + 1):
                    if level <= 3:
                        value = jnp.sum(jnp.where(hit[level], term, 0.0), axis=0, keepdims=True)
                    else:
                        size = 1 << (level - 1)
                        value = jnp.zeros((1, LANES), F32)
                        for odd in range(1, Q // size, 2):
                            rows = jnp.sum(term[odd * size : (odd + 1) * size], axis=0, keepdims=True)
                            value = jnp.where(lane // size == odd - 1, rows, value)
                    tab[k * levels + level, pl.ds(p * per + j, 1), :] = value
        return carry

    def far_maps(p):
        for c in range(2):
            cs = []
            for k in range(2):
                value = fcs[k, p]
                if c == 1:
                    value = value + wrow(p, k, mid) * s0[p]
                cs.append(value.astype(BF16))
            cs = jnp.concatenate(cs, axis=0)
            src = fsrc[p]
            if c == 0:
                src = src + wrow(p, 0, mid) * q1[0, p] + wrow(p, 1, mid) * q1[1, p]
            src = src.astype(BF16)
            class_b[c, p] = cs
            source_b[c, p] = src
            in_acc[c] = in_acc[c] + dot(scaled[p, spans[c], :], src, 1, 1)
            out_acc[c] = out_acc[c] + dot(g_ref[spans[c], cols(p)], cs, 1, 1)

    def far_values(p):
        for c in range(2):
            cs = class_b[c, p]
            src = source_b[c, p]
            read = dot(mo2[c], cs, 1, 0)
            out_ref[spans[c], cols(p)] = (nout[p, spans[c], :] + read).astype(BF16)
            vg = dot(bin_ref[spans[c], :], src, 1, 0)
            xg_ref[spans[c], cols(p)] = (
                nback[p, spans[c], :] + stepx[p, spans[c], :] * vg
            ).astype(BF16)
            picks = jnp.concatenate(half_f + [jnp.zeros((8 - per, LANES), F32)], axis=0)
            far_step = dot(picks, x_ref[spans[c], cols(p)].astype(F32) * vg, 1, 1, HIGH)
            for j in range(per):
                at = (p * per + j, slice(c, c + 1), slice(None))
                sgrow[at] = sgrow[at] + far_step[j : j + 1]

    lag = 2

    def pipeline(i, carry):
        last = i - lag * (nb - 1)

        @pl.when(last > 0)
        def _():
            far_values(last - 1)

        @pl.when(i < pairs)
        def _():
            near(i, 0)

        for b in range(nb):
            p = i - lag * b

            @pl.when((p >= 0) & (p < pairs))
            def _(b=b, p=p):
                combine(b, p)
                if b + 1 < nb:
                    start(b + 1, p)
                else:
                    far_maps(p)

        return carry

    lax.fori_loop(0, pairs + lag * (nb - 1), pipeline, 0)

    grads = [[], []]
    for c in range(2):
        sgb = score_sum[c].astype(BF16)
        is_one = clsb[spans[c], :] > 0.5
        acc = out_acc[c]
        grads[0].append(in_acc[c] + dot(sgb, cout_ref[spans[c], :], 0, 0))
        grads[1].append(
            jnp.where(is_one, acc[:, state:], acc[:, :state])
            + dot(sgb, bin_ref[spans[c], :], 1, 0)
        )
    full = jnp.concatenate(grads[0] + grads[1], axis=0)
    rows = 2 * tokens // n_head
    for q in range(n_head):
        part_own[q] = full[q * rows : (q + 1) * rows]
        part_send[q] = full[q * rows : (q + 1) * rows].astype(BF16)

    def part_copy(i):
        to = lax.rem(mine + i, n_head)
        return pltpu.make_async_remote_copy(
            part_send.at[to], part_recv.at[i], p_ssem.at[i], p_rsem.at[i],
            device_id={"head": to}, device_id_type=MESH,
        )

    def all_copy(i, slot):
        to = lax.rem(mine + i, n_head)
        return pltpu.make_async_remote_copy(
            final.at[slot], final.at[slot], a_ssem.at[i], a_rsem.at[i],
            device_id={"head": to}, device_id_type=MESH,
        )

    for i in range(1, n_head):
        part_copy(i).start()
    def table_copy(i):
        return pltpu.make_async_remote_copy(
            tsend, trecv.at[i], t_ssem.at[i], t_rsem.at[i],
            device_id={"seq": device ^ i}, device_id_type=MESH,
        )

    table_sum = []
    for k in range(2):
        acc = jnp.zeros((heads, LANES), F32)
        for level in range(levels):
            col = jnp.sum(tab[k * levels + level], axis=1, keepdims=True)
            acc = jnp.where(lane == level, col * (scale_of(level) / math.sqrt(total)), acc)
        table_sum.append(acc)
    for k in range(2):
        tsend[k, :heads, :] = table_sum[k]
        trecv[0, k, :heads, :] = table_sum[k]
    for i in range(1, 1 << nb):
        table_copy(i).start()

    far_values(pairs - 1)
    for h in range(heads):
        for c in range(2):
            sg_ref[h : h + 1, spans[c]] = sgrow[h, c : c + 1, :]
    summed = part_own[mine]
    for i in range(1, n_head):
        part_copy(i).wait_recv()
        summed = summed + part_recv[i].astype(F32)
    final[mine] = summed.astype(BF16)
    for i in range(1, n_head):
        all_copy(i, mine).start()
    for i in range(1, 1 << nb):
        table_copy(i).wait_recv()
    for k in range(2):
        table_sum[k] = trecv[device, k, :heads, :]
        for owner in range(1, 1 << nb):
            table_sum[k] = table_sum[k] + trecv[device ^ owner, k, :heads, :]
    for k in range(2):
        tg_ref[:, k, :] = table_sum[k][:, :levels]
    for i in range(1, n_head):
        all_copy(i, lax.rem(mine + n_head - i, n_head)).wait_recv()
    per_out = n_head // 2
    for q in range(n_head):
        where = (slice((q % per_out) * rows, (q % per_out + 1) * rows), slice(None))
        (ing_ref if q < per_out else outg_ref)[where] = final[q].astype(F32)

    for i in range(1, n_head):
        part_copy(i).wait_send()
        all_copy(i, mine).wait_send()
    for i in range(1, 1 << nb):
        table_copy(i).wait_send()
    for b in range(nb):

        def drain(p, carry, b=b):
            @pl.when(f_sent[b])
            def _():
                f_copy(b, p).wait_send()

            @pl.when(c_sent[b])
            def _():
                r_copy(b, 0, p).wait_send()

            @pl.when(r_one[b])
            def _():
                r_copy(b, 1, p).wait_send()

            @pl.when(r_both[b])
            def _():
                for k in range(2):
                    r_copy(b, k, p).wait_send()

            return carry

        lax.fori_loop(0, pairs, drain, 0)


def write_out(*refs):
    sem = refs[-1]
    copies = [pltpu.make_async_copy(refs[i], refs[6 + i], sem.at[i]) for i in range(6)]
    for copy in copies:
        copy.start()
    for copy in copies:
        copy.wait()


def local(inputs, step_sizes, input_map, output_map, level_table, token_class, cotangent):
    tokens, state = input_map.shape
    heads = step_sizes.shape[0]
    width = inputs.shape[1] // heads
    levels = level_table.shape[2]
    n_seq = lax.axis_size("seq")
    n_head = lax.axis_size("head")
    nb = n_seq.bit_length() - 1
    per = LANES // width
    pairs = heads // per
    assert tokens == 2 * Q and heads % per == 0 and n_head % 2 == 0 and nb > 0
    assert level_table.shape[1] == 2 and state == Q
    dims = (heads, width, tokens, state, levels, nb, n_head, float(tokens * n_seq))
    rows = 2 * tokens // n_head
    vmem = pl.BlockSpec(memory_space=pltpu.VMEM)
    hbm = pl.BlockSpec(memory_space=pltpu.HBM)
    dma = pltpu.SemaphoreType.DMA
    unit = (pairs, state, LANES)
    tall = (pairs, tokens, LANES)
    padded = -(-heads // 8) * 8
    placed = [
        pltpu.with_memory_space_constraint(a, pltpu.HBM)
        for a in (
            inputs, step_sizes, input_map, output_map, level_table,
            token_class.reshape(1, tokens), cotangent,
        )
    ]
    results = pl.pallas_call(
        functools.partial(kernel, dims),
        out_shape=(
            jax.ShapeDtypeStruct(inputs.shape, BF16),
            jax.ShapeDtypeStruct(inputs.shape, BF16),
            jax.ShapeDtypeStruct(step_sizes.shape, F32),
            jax.ShapeDtypeStruct(input_map.shape, F32),
            jax.ShapeDtypeStruct(output_map.shape, F32),
            jax.ShapeDtypeStruct(level_table.shape, F32),
        ),
        in_specs=[hbm] * 7,
        out_specs=(vmem,) * 6,
        scratch_shapes=[
            pltpu.VMEM(tall, F32),
            pltpu.VMEM(tall, BF16),
            pltpu.VMEM((tokens, LANES), F32),
            pltpu.VMEM((Q, Q), jnp.int32),
            pltpu.VMEM((2, Q, Q), F32),
            pltpu.VMEM((2, Q, 2 * state), BF16),
            pltpu.VMEM(unit, F32),
            pltpu.VMEM((2, *unit), F32),
            pltpu.VMEM((2, *unit), F32),
            pltpu.VMEM(unit, F32),
            pltpu.VMEM((2, *unit), F32),
            pltpu.VMEM((2, *unit), F32),
            pltpu.VMEM(unit, F32),
            pltpu.VMEM(tall, F32),
            pltpu.VMEM(tall, F32),
            pltpu.VMEM((2, Q, Q), F32),
            pltpu.VMEM((2, Q, state), F32),
            pltpu.VMEM((2, Q, 2 * state), F32),
            pltpu.VMEM((2 * levels, heads, LANES), F32),
            pltpu.VMEM((nb, *unit), BF16),
            pltpu.VMEM((nb, *unit), BF16),
            pltpu.VMEM((nb, 2, *unit), BF16),
            pltpu.VMEM((nb, 2, *unit), BF16),
            pltpu.VMEM((n_head, rows, state), BF16),
            pltpu.VMEM((n_head, rows, state), BF16),
            pltpu.VMEM((n_head, rows, state), F32),
            pltpu.VMEM((n_head, rows, state), BF16),
            pltpu.VMEM((2, padded, LANES), F32),
            pltpu.VMEM((n_seq, 2, padded, LANES), F32),
            dma((nb, pairs)),
            dma((nb, pairs)),
            dma((nb, 2, pairs)),
            dma((nb, 2, pairs)),
            dma((n_head,)),
            dma((n_head,)),
            dma((n_head,)),
            dma((n_head,)),
            dma((n_seq,)),
            dma((n_seq,)),
            pltpu.VMEM((heads, 2, LANES), F32),
            pltpu.VMEM((heads, 2, LANES), F32),
            pltpu.VMEM((2, pairs, 2 * state, LANES), BF16),
            pltpu.VMEM((2, *unit), BF16),
            pltpu.VMEM(inputs.shape, BF16),
            pltpu.VMEM(step_sizes.shape, F32),
            pltpu.VMEM(input_map.shape, BF16),
            pltpu.VMEM(output_map.shape, BF16),
            pltpu.VMEM((1, tokens), jnp.int32),
            pltpu.VMEM(cotangent.shape, BF16),
            pltpu.SMEM(level_table.shape, F32),
            dma((7,)),
        ],
        compiler_params=pltpu.CompilerParams(
            collective_id=0, has_side_effects=True, vmem_limit_bytes=48 << 20
        ),
    )(*placed)
    return pl.pallas_call(
        write_out,
        out_shape=tuple(jax.ShapeDtypeStruct(r.shape, r.dtype) for r in results),
        in_specs=[vmem] * 6,
        out_specs=(hbm,) * 6,
        scratch_shapes=[dma((6,))],
        compiler_params=pltpu.CompilerParams(vmem_limit_bytes=8 << 20),
    )(*results)


def solution(mesh):
    placed = (
        P("seq", "head"),
        P("head", "seq"),
        P("seq", None),
        P("seq", None),
        P("head", None, None),
        P("seq"),
        P("seq", "head"),
    )
    return jax.shard_map(
        local,
        mesh=mesh,
        in_specs=placed,
        out_specs=(
            P("seq", "head"),
            P("seq", "head"),
            P("head", "seq"),
            P("seq", None),
            P("seq", None),
            P("head", None, None),
        ),
        check_vma=False,
    )
```
